32 devices in a mesh: member: 2 (over x), wave: 16 (over z, y, core).
Axes of the slice: x: 2, y: 2, z: 4, core: 2. Of those that a mesh axis runs over, the one named last changes fastest.
Arguments:
- spectral: bfloat16 [1024, 2, 256, 192], P(('member', 'wave')), parts along dimension 0, may hold values from -6 to 6
- basis: bfloat16 [512, 2, 256, 256], P('wave'), may hold values from -0.25 to 0.25
- quad_weights: float32 [256], replicated, may hold values from 0.5 to 2
- column: float32 [96, 96], replicated, may hold values from -0.625 to 0.625
- square_coef: float32 [96], replicated, may hold values from -0.3 to 0.3
- cube_coef: float32 [96], replicated, may hold values from 0.05 to 0.2
- trunc: int32 [256], replicated, may hold values from 16 to 512, as said below
Outputs:
- new_spectral: bfloat16 [1024, 2, 256, 192], P(('member', 'wave')), parts along dimension 0
The draws below stay inside these ranges and needn't reach their ends.
There are 2 independent parts, one for each index of `member`. The reference program is written for one: setup_inputs(seed, part) draws one part's arguments, and reference() takes and returns one part's arrays. A program takes and returns all parts, laid end to end along the dimension named above; an argument that names none is the same for every part. Nothing has to cross between parts.
Inputs may be any that keep to these rules, and one draw needn't show every extreme that they name: `trunc`: rows nearer the equator never keep fewer wavenumbers than rows nearer the pole.
All inputs are finite; a program needn't handle non-finite values.
Results may differ from the reference program's by a relative error of at most 0.0057.
Values may be sent and summed in bfloat16 or wider, within the bound.
No kernel may reach another device: no remote copies, remote signals or barrier semaphores. Data moves between devices by JAX's collectives and lax.ppermute only.
A program may use at most 128 MiB of HBM per device.

```python
import math
import jax
import jax.numpy as jnp
from jax import lax

WAVES = 512
DEGREES = 512
HALF_DEG = 256
HLAT = 256
NLAT = 512
NLON = 1024
LEV = 96


def draw_trunc(key, part):
    increments = jax.random.randint(key, (HLAT,), 0, 4)
    climbing = 16 + jnp.cumsum(increments)
    row_ids = jnp.arange(HLAT)
    equator_band = jnp.where(row_ids >= HLAT - HLAT // 8, WAVES, 0)
    return jnp.minimum(jnp.maximum(climbing, equator_band), WAVES).astype(jnp.int32)


def block_scale(rng, extent, cuts, smallest, largest):
    gain, own = 1.0, jax.random.fold_in(rng, 6)
    for axis_at, blocks in cuts:
        draws = jnp.exp(jax.random.uniform(jax.random.fold_in(own, axis_at), (blocks,), jnp.float32, smallest / len(cuts), largest / len(cuts)))
        gain = gain * jnp.repeat(draws, extent[axis_at] // blocks).reshape([-1 if axis == axis_at else 1 for axis in range(len(extent))])
    return gain


def gaussian(own_key, dims, width, limit, shards=(), kind=jnp.bfloat16):
    gain = block_scale(own_key, dims, shards, -0.22, 0.18) if shards else 1.0
    array = jax.random.normal(own_key, dims, jnp.float32) * width * gain
    return jnp.minimum(jnp.maximum(array, -limit), limit).astype(kind)


def setup_inputs(seed: int = 0, part: int = 0) -> dict:
    keys = jax.random.split(jax.random.key(seed), 8)
    part_keys = jax.random.split(jax.random.fold_in(keys[7], part), 8)
    return {
        "spectral": gaussian(part_keys[0], (WAVES, 2, HALF_DEG, 2 * LEV), 1.0, 6.0, ((0, 16),)),
        "basis": gaussian(keys[1], (WAVES, 2, HALF_DEG, HLAT), DEGREES ** -0.5, 0.25, ((0, 16),)),
        "quad_weights": jnp.clip(jnp.exp(jax.random.uniform(keys[2], (HLAT,), jnp.float32, math.log(0.5), math.log(2.0))), 0.5, 2.0),
        "column": gaussian(keys[3], (LEV, LEV), LEV ** -0.5, 0.625, (), jnp.float32),
        "square_coef": jnp.clip(jax.random.uniform(keys[4], (LEV,), jnp.float32, -0.3, 0.3), -0.3, 0.3),
        "cube_coef": jnp.clip(jnp.exp(jax.random.uniform(keys[5], (LEV,), jnp.float32, math.log(0.05), math.log(0.2))), 0.05, 0.2),
        "trunc": draw_trunc(jax.random.fold_in(keys[7], 71), part),
    }


def fourier_table():
    wave_ids = jnp.arange(WAVES, dtype=jnp.int32)
    lon_ids = jnp.arange(NLON, dtype=jnp.int32)
    phases = wave_ids[:, None] * lon_ids[None, :] % NLON
    angles = phases.astype(jnp.float32) * (2.0 * math.pi / NLON)
    return jnp.stack([jnp.cos(angles), -jnp.sin(angles)], axis=1).astype(jnp.bfloat16)

def inverse_wave(pieces):
    basis_m, spec_m = pieces
    return jnp.einsum('pkj,pkc->pjc', basis_m.astype(jnp.float32), spec_m.astype(jnp.float32))

def direct_wave(pieces):
    basis_m, fold_m = pieces
    return jnp.einsum('pkj,pjc->pkc', basis_m.astype(jnp.float32), fold_m.astype(jnp.float32))

def reference(spectral, basis, quad_weights, column, square_coef, cube_coef, trunc):
    degrees = jnp.arange(WAVES, dtype=jnp.int32)[:, None, None] + 2 * jnp.arange(HALF_DEG, dtype=jnp.int32)[None, None, :] + jnp.arange(2, dtype=jnp.int32)[None, :, None]
    in_range = (degrees < DEGREES)[..., None]
    spec_in = jnp.where(in_range, spectral, jnp.zeros_like(spectral))
    parities = lax.map(inverse_wave, (basis, spec_in))
    north_rows = parities[:, 0] + parities[:, 1]
    south_rows = parities[:, 0] - parities[:, 1]
    coeffs = jnp.concatenate([north_rows, south_rows[:, ::-1]], axis=1).astype(jnp.bfloat16)
    row_lats = jnp.concatenate([jnp.arange(HLAT, dtype=jnp.int32), jnp.arange(HLAT, dtype=jnp.int32)[::-1]])
    kept_mask = (jnp.arange(WAVES, dtype=jnp.int32)[:, None] < trunc[row_lats][None, :])[..., None]
    coeffs = jnp.where(kept_mask, coeffs, jnp.zeros_like(coeffs))
    fourier = fourier_table().astype(jnp.float32)
    lat_block = 16
    blocks = NLAT // lat_block
    coeff_blocks = coeffs.reshape(WAVES, blocks, lat_block, 2, LEV).transpose(1, 0, 2, 3, 4)

    def synthesise(block):
        grid_temp = jnp.einsum('mgrv,mrx->gvx', block.astype(jnp.float32), fourier) * (1.0 / math.sqrt(WAVES))
        column_mix = jnp.einsum('uv,gvx->gux', column, grid_temp, precision=lax.Precision.HIGHEST)
        return column_mix + square_coef[None, :, None] * grid_temp * grid_temp - cube_coef[None, :, None] * grid_temp * grid_temp * grid_temp
    tendency = lax.map(synthesise, coeff_blocks).reshape(NLAT, LEV, NLON)
    weight_rows = quad_weights[row_lats]
    level_mean = lax.optimization_barrier(jnp.sum(tendency * weight_rows[:, None, None], axis=(0, 2))) / (NLON * 2.0 * jnp.sum(quad_weights))
    shifted = (tendency - level_mean[None, :, None]).astype(jnp.bfloat16)

    def analyse(block):
        return jnp.einsum('gvx,mrx->mgrv', block.astype(jnp.float32), fourier) * math.sqrt(2.0 / NLON)
    analysed = lax.map(analyse, shifted.reshape(blocks, lat_block, LEV, NLON))
    analysed = analysed.transpose(1, 0, 2, 3, 4).reshape(WAVES, NLAT, 2 * LEV)
    analysed = jnp.where(kept_mask, analysed, 0.0).astype(jnp.bfloat16)
    settled = lax.optimization_barrier(analysed).astype(jnp.float32)
    north_back = settled[:, :HLAT]
    south_back = settled[:, HLAT:][:, ::-1]
    weight = quad_weights[None, :, None]
    folded = jnp.stack([weight * (north_back + south_back), weight * (north_back - south_back)], axis=1).astype(jnp.bfloat16)
    direct = lax.map(direct_wave, (basis, folded))
    return jnp.where(in_range, spec_in.astype(jnp.float32) + direct, 0.0).astype(jnp.bfloat16)
```

```python
import functools
import math

import jax
import jax.numpy as jnp
from jax import lax
from jax.experimental import pallas as pl
from jax.experimental.pallas import tpu as pltpu
from jax.sharding import PartitionSpec as P

NLON = 1024
LANES = 128
F32 = jnp.float32
BF16 = jnp.bfloat16
VMEM_LIMIT = 56 * 1024 * 1024


def params():
    return pltpu.CompilerParams(
        dimension_semantics=("arbitrary",), vmem_limit_bytes=VMEM_LIMIT
    )


def latitude_order(half_lats, devices):
    rows = half_lats // devices
    pairs = rows // 2
    lane = jnp.arange(half_lats, dtype=jnp.int32)
    half = lane // (half_lats // 2)
    owner = lane % (half_lats // 2) // pairs
    pair = lane % pairs
    return (devices - 1 - owner) * rows + half * pairs + pair


def forward_kernel(devices, group, waves, pos_ref, spec_ref, basis_ref, trunc_ref, perm_ref, *rest):
    outs, fold = rest[:devices], rest[devices:]
    pos = pos_ref[0]
    levels = outs[0].shape[3] // 4
    half_slots = spec_ref.shape[3]
    tiles = 4 * levels // LANES
    jj = perm_ref.shape[1] // 2
    pairs = jj // devices
    first = pos * waves + pl.program_id(0) * group
    slot = 2 * lax.broadcasted_iota(jnp.int32, (1, half_slots), 1)
    trunc = trunc_ref[...]

    def one(m, carry):
        wave = first + m
        parity = []
        for p in range(2):
            spec = spec_ref[m, p]
            spec = jnp.where(slot + (wave + p) < 2 * half_slots, spec, jnp.zeros_like(spec))
            parity.append(jnp.dot(spec, basis_ref[m, p], preferred_element_type=F32))
        both = jnp.concatenate([parity[0] + parity[1], parity[0] - parity[1]], axis=0)
        both = jnp.where(trunc > wave, both, 0.0).astype(BF16)
        both = jnp.dot(both, perm_ref[...], preferred_element_type=F32)
        for r in range(2):
            rows = []
            for half in range(2):
                for hemi in range(2):
                    at = (2 * hemi + r) * levels
                    rows.append(both[at : at + levels, half * jj : (half + 1) * jj])
            turned = jnp.concatenate(rows, axis=0).T
            for t in range(tiles):
                at = pl.ds(m, jj, stride=group)
                fold[r * tiles + t][at, :] = turned[:, t * LANES : (t + 1) * LANES]
        return carry

    lax.fori_loop(0, group, one, 0)
    size = pairs * group
    for s in range(devices):
        at = pl.multiple_of((pos ^ s) * size, 8)
        for r in range(2):
            for t in range(tiles):
                block = fold[r * tiles + t][pl.ds(at, size), :].reshape(pairs, group, LANES)
                outs[s][:, r, :, t * LANES : (t + 1) * LANES] = block.astype(BF16)


def forward(pos, spec, basis, trunc, perm, devices):
    waves, _, channels, half_slots = spec.shape
    half_lats = basis.shape[3]
    group = min(8, waves)
    pairs = half_lats // (2 * devices)
    lanes = 2 * channels
    return pl.pallas_call(
        functools.partial(forward_kernel, devices, group, waves),
        grid_spec=pltpu.PrefetchScalarGridSpec(
            num_scalar_prefetch=1,
            grid=(waves // group,),
            in_specs=[
                pl.BlockSpec((group, 2, channels, half_slots), lambda i, s: (i, 0, 0, 0)),
                pl.BlockSpec((group, 2, half_slots, half_lats), lambda i, s: (i, 0, 0, 0)),
                pl.BlockSpec((1, half_lats), lambda i, s: (0, 0)),
                pl.BlockSpec((half_lats, half_lats), lambda i, s: (0, 0)),
            ],
            out_specs=[pl.BlockSpec((pairs, 2, group, lanes), lambda i, s: (0, 0, i, 0))] * devices,
            scratch_shapes=[pltpu.VMEM((half_lats // 2 * group, LANES), F32)] * (2 * lanes // LANES),
        ),
        out_shape=[jax.ShapeDtypeStruct((pairs, 2, waves, lanes), BF16)] * devices,
        compiler_params=params(),
        name="forward",
    )(pos, spec, basis, trunc, perm)


def synth_kernel(devices, waves, scale, pos_ref, table_ref, mix_ref, coef_ref, *rest):
    blocks = rest[:devices]
    out_ref, mean_ref, coeffs, tend = rest[devices:]
    pos = pos_ref[0]
    total = devices * waves
    for s in range(devices):
        at = pl.multiple_of((pos ^ s) * waves, 8)
        for r in range(2):
            coeffs[pl.ds(r * total + at, waves), :] = blocks[s][0, r]
    lons = table_ref.shape[0]
    step = lons // 4

    def one(t, total_sum):
        at = pl.multiple_of(t * step, step)
        temp = scale * jnp.dot(
            table_ref[pl.ds(at, step), :], coeffs[...], preferred_element_type=F32
        )
        high = temp.astype(BF16)
        mixed = jnp.dot(high, mix_ref[...], preferred_element_type=F32)
        value = mixed + temp * temp * (coef_ref[0:1, :] - coef_ref[1:2, :] * temp)
        tend[pl.ds(at, step), :] = value
        return total_sum + jnp.sum(value, axis=0, keepdims=True)

    zero = jnp.zeros((1, out_ref.shape[2]), F32)
    mean = lax.fori_loop(0, 4, one, zero) * (1.0 / lons)
    mean_ref[0] = jnp.broadcast_to(mean, mean_ref.shape[1:])

    def two(t, carry):
        at = pl.multiple_of(t * step, step)
        out_ref[0, pl.ds(at, step), :] = (tend[pl.ds(at, step), :] - mean).astype(BF16)
        return carry

    lax.fori_loop(0, 4, two, 0)


def synthesise(pos, table, mix, coef, blocks):
    devices = len(blocks)
    pairs, _, waves, lanes = blocks[0].shape
    lons, depth = table.shape
    return pl.pallas_call(
        functools.partial(synth_kernel, devices, waves, 1.0 / math.sqrt(devices * waves)),
        grid_spec=pltpu.PrefetchScalarGridSpec(
            num_scalar_prefetch=1,
            grid=(pairs,),
            in_specs=[
                pl.BlockSpec((lons, depth), lambda q, s: (0, 0)),
                pl.BlockSpec((lanes, lanes), lambda q, s: (0, 0)),
                pl.BlockSpec((2, lanes), lambda q, s: (0, 0)),
            ]
            + [pl.BlockSpec((1, 2, waves, lanes), lambda q, s: (q, 0, 0, 0))] * devices,
            out_specs=[
                pl.BlockSpec((1, lons, lanes), lambda q, s: (q, 0, 0)),
                pl.BlockSpec((1, 8, lanes), lambda q, s: (q, 0, 0)),
            ],
            scratch_shapes=[pltpu.VMEM((depth, lanes), BF16), pltpu.VMEM((lons, lanes), F32)],
        ),
        out_shape=[
            jax.ShapeDtypeStruct((pairs, lons, lanes), BF16),
            jax.ShapeDtypeStruct((pairs, 8, lanes), F32),
        ],
        compiler_params=params(),
        name="synthesise",
    )(pos, table, mix, coef, *blocks)


def analyse_kernel(devices, waves, scale, pos_ref, table_ref, sums_ref, shifted_ref, excess_ref, *rest):
    outs, full = rest[:devices], rest[devices]
    pos = pos_ref[0]
    total = devices * waves
    depth = table_ref.shape[0]
    step = depth // 4
    excess = excess_ref[0, 0:1, :]

    def one(t, carry):
        at = pl.multiple_of(t * step, step)
        value = jnp.dot(table_ref[pl.ds(at, step), :], shifted_ref[0], preferred_element_type=F32)
        value = value + sums_ref[pl.ds(at, step), :] * excess
        full[pl.ds(at, step), :] = (scale * value).astype(BF16)
        return carry

    lax.fori_loop(0, 4, one, 0)
    for s in range(devices):
        at = pl.multiple_of((pos ^ s) * waves, 8)
        for r in range(2):
            outs[s][0, r] = full[pl.ds(r * total + at, waves), :]


def analyse(pos, table, sums, shifted, excess, devices, waves):
    pairs, lons, lanes = shifted.shape
    depth = table.shape[0]
    return pl.pallas_call(
        functools.partial(analyse_kernel, devices, waves, math.sqrt(2.0 / lons)),
        grid_spec=pltpu.PrefetchScalarGridSpec(
            num_scalar_prefetch=1,
            grid=(pairs,),
            in_specs=[
                pl.BlockSpec((depth, lons), lambda q, s: (0, 0)),
                pl.BlockSpec((depth, 1), lambda q, s: (0, 0)),
                pl.BlockSpec((1, lons, lanes), lambda q, s: (q, 0, 0)),
                pl.BlockSpec((1, 8, lanes), lambda q, s: (q, 0, 0)),
            ],
            out_specs=[pl.BlockSpec((1, 2, waves, lanes), lambda q, s: (q, 0, 0, 0))] * devices,
            scratch_shapes=[pltpu.VMEM((depth, lanes), BF16)],
        ),
        out_shape=[jax.ShapeDtypeStruct((pairs, 2, waves, lanes), BF16)] * devices,
        compiler_params=params(),
        name="analyse",
    )(pos, table, sums, shifted, excess)


def inverse_kernel(devices, group, waves, pos_ref, spec_ref, basis_ref, trunc_ref, weight_ref, perm_ref, *rest):
    blocks = rest[:devices]
    out_ref, fold = rest[devices], rest[devices + 1 :]
    pos = pos_ref[0]
    levels = blocks[0].shape[3] // 4
    half_slots = spec_ref.shape[3]
    jj = perm_ref.shape[0] // 2
    pairs = jj // devices
    tiles = 4 * levels // LANES
    size = pairs * group
    for s in range(devices):
        at = pl.multiple_of((pos ^ s) * size, 8)
        for r in range(2):
            for t in range(tiles):
                block = blocks[s][:, r, :, t * LANES : (t + 1) * LANES].astype(F32)
                fold[r * tiles + t][pl.ds(at, size), :] = block.reshape(size, LANES)
    first = pos * waves + pl.program_id(0) * group
    slot = 2 * lax.broadcasted_iota(jnp.int32, (1, half_slots), 1)
    trunc = trunc_ref[...]
    weight = weight_ref[...]

    def one(m, carry):
        wave = first + m
        turned = []
        for r in range(2):
            at = pl.ds(m, jj, stride=group)
            columns = [fold[r * tiles + t][at, :].T for t in range(tiles)]
            turned.append(jnp.concatenate(columns, axis=0))
        rows = []
        for hemi in range(2):
            for r in range(2):
                pieces = []
                for half in range(2):
                    at = (2 * half + hemi) * levels
                    pieces.append(turned[r][at : at + levels])
                rows.append(jnp.concatenate(pieces, axis=1))
        both = jnp.concatenate(rows, axis=0).astype(BF16)
        both = jnp.dot(both, perm_ref[...], preferred_element_type=F32)
        both = jnp.where(trunc > wave, both, 0.0)
        channels = 2 * levels
        north, south = both[:channels], both[channels:]
        for p in range(2):
            folded = (weight * (north + south if p == 0 else north - south)).astype(BF16)
            direct = lax.dot_general(
                folded, basis_ref[m, p], (((1,), (1,)), ((), ())), preferred_element_type=F32
            )
            value = spec_ref[m, p].astype(F32) + direct
            out_ref[m, p] = jnp.where(slot + (wave + p) < 2 * half_slots, value, 0.0).astype(BF16)
        return carry

    lax.fori_loop(0, group, one, 0)


def inverse(pos, spec, basis, trunc, weight, perm, blocks):
    devices = len(blocks)
    waves, _, channels, half_slots = spec.shape
    half_lats = basis.shape[3]
    group = min(8, waves)
    pairs = half_lats // (2 * devices)
    lanes = 2 * channels
    return pl.pallas_call(
        functools.partial(inverse_kernel, devices, group, waves),
        grid_spec=pltpu.PrefetchScalarGridSpec(
            num_scalar_prefetch=1,
            grid=(waves // group,),
            in_specs=[
                pl.BlockSpec((group, 2, channels, half_slots), lambda i, s: (i, 0, 0, 0)),
                pl.BlockSpec((group, 2, half_slots, half_lats), lambda i, s: (i, 0, 0, 0)),
                pl.BlockSpec((1, half_lats), lambda i, s: (0, 0)),
                pl.BlockSpec((1, half_lats), lambda i, s: (0, 0)),
                pl.BlockSpec((half_lats, half_lats), lambda i, s: (0, 0)),
            ]
            + [pl.BlockSpec((pairs, 2, group, lanes), lambda i, s: (0, 0, i, 0))] * devices,
            out_specs=pl.BlockSpec((group, 2, channels, half_slots), lambda i, s: (i, 0, 0, 0)),
            scratch_shapes=[pltpu.VMEM((half_lats // 2 * group, LANES), F32)] * (2 * lanes // LANES),
        ),
        out_shape=jax.ShapeDtypeStruct(spec.shape, BF16),
        compiler_params=params(),
        name="inverse",
    )(pos, spec, basis, trunc, weight, perm, *blocks)


def cos_sin(rows, columns):
    phases = rows[:, None] * columns[None, :] % NLON
    angles = phases.astype(F32) * (2.0 * math.pi / NLON)
    return jnp.cos(angles), jnp.sin(angles)


def fourier_tables(waves, lons):
    def outer(rows, columns):
        low = 32
        col = jnp.arange(columns, dtype=jnp.int32)
        small = lax.optimization_barrier(
            cos_sin(jnp.arange(low, dtype=jnp.int32), col)
            + cos_sin(low * jnp.arange(rows // low, dtype=jnp.int32), col)
        )
        c0, s0, c1, s1 = small
        cos = c1[:, None] * c0[None] - s1[:, None] * s0[None]
        sin = s1[:, None] * c0[None] + c1[:, None] * s0[None]
        return cos.reshape(rows, columns).astype(BF16), (-sin).reshape(rows, columns).astype(BF16)

    analysis = jnp.concatenate(outer(waves, lons), axis=0)
    synthesis = jnp.concatenate(outer(lons, waves), axis=1)
    return synthesis, analysis


def exchange(arrays, devices, needed):
    got = [arrays[0]]
    for s in range(1, devices):
        pairs = [(i, i ^ s) for i in range(devices) if needed(i, i ^ s)]
        got.append(lax.ppermute(arrays[s], "wave", pairs))
    return got


def sum_over_wave(value, devices):
    span = 1
    while span < devices:
        others = [k * span for k in range(1, 4) if k * span < devices]
        moved = [
            lax.ppermute(value, "wave", [(i, i ^ k) for i in range(devices)]) for k in others
        ]
        for part in moved:
            value = value + part
        span *= 4
    return value


def per_device(spectral, basis, quad_weights, column, square_coef, cube_coef, trunc):
    devices = lax.axis_size("wave")
    position = lax.axis_index("wave").astype(jnp.int32)
    waves, _, half_slots, channels = spectral.shape
    half_lats = basis.shape[3]
    levels = channels // 2
    rows = half_lats // devices
    pairs = rows // 2
    pos = position.reshape(1)
    spec = jnp.swapaxes(spectral, 2, 3)
    order = latitude_order(half_lats, devices)
    lats = jnp.arange(half_lats, dtype=jnp.int32)
    perm = (lats[:, None] == order[None, :]).astype(BF16)
    back = (order[:, None] == lats[None, :]).astype(BF16)
    trunc_row = trunc.reshape(1, half_lats)
    weight_row = quad_weights.reshape(1, half_lats)
    blocks = forward(pos, spec, basis, trunc_row, perm, devices)

    reach = [min(devices, g + 1 + max(1, devices // 16)) for g in range(devices)]
    top = jnp.max(trunc.reshape(devices, rows), axis=1)
    fits = jnp.all(top <= waves * jnp.array(reach, dtype=jnp.int32))

    def finish(sparse, blocks):
        def there(source, owner):
            return not sparse or source < reach[devices - 1 - owner]

        def home(owner, source):
            return there(source, owner)

        synthesis, analysis = fourier_tables(devices * waves, NLON)
        sums = jnp.sum(analysis.astype(F32), axis=1, keepdims=True)
        mix = jnp.kron(jnp.eye(4, dtype=F32), column.T).astype(BF16)
        coef = jnp.stack([jnp.tile(square_coef, 4), jnp.tile(cube_coef, 4)])
        group = devices - 1 - position
        own = lax.dynamic_slice(quad_weights, (group * rows,), (rows,)).reshape(2, pairs)
        own = own.T[:, :, None, None]
        norm = 1.0 / (2.0 * jnp.sum(quad_weights))

        got = exchange(blocks, devices, there)
        shifted, means = synthesise(pos, synthesis, mix, coef, got)
        zonal = means[:, 0].reshape(pairs, 2, 2, levels)
        level_mean = sum_over_wave(jnp.sum(own * zonal, axis=(0, 1, 2)), devices) * norm
        excess = means - jnp.tile(level_mean, 4)
        parts = analyse(pos, analysis, sums, shifted, excess, devices, waves)
        parts = exchange(parts, devices, home)
        return inverse(pos, spec, basis, trunc_row, weight_row, back, parts)

    out = lax.cond(
        fits, functools.partial(finish, True), functools.partial(finish, False), blocks
    )
    return jnp.swapaxes(out, 2, 3)


def solution(mesh):
    return jax.shard_map(
        per_device,
        mesh=mesh,
        in_specs=(
            P(("member", "wave"), None, None, None),
            P("wave", None, None, None),
            P(),
            P(),
            P(),
            P(),
            P(),
        ),
        out_specs=P(("member", "wave"), None, None, None),
        check_vma=False,
    )
```

```python
import functools
import math

import jax
import jax.numpy as jnp
from jax import lax
from jax.experimental import pallas as pl
from jax.experimental.pallas import tpu as pltpu
from jax.sharding import PartitionSpec as P

NLON = 1024
LANES = 128
F32 = jnp.float32
BF16 = jnp.bfloat16
VMEM_LIMIT = 56 * 1024 * 1024


def params():
    return pltpu.CompilerParams(
        dimension_semantics=("arbitrary",), vmem_limit_bytes=VMEM_LIMIT
    )


def latitude_order(half_lats, devices):
    rows = half_lats // devices
    pairs = rows // 2
    lane = jnp.arange(half_lats, dtype=jnp.int32)
    half = lane // (half_lats // 2)
    owner = lane % (half_lats // 2) // pairs
    pair = lane % pairs
    return (devices - 1 - owner) * rows + half * pairs + pair


def exchange_order(devices):
    half = devices // 2
    far = sorted(range(half, devices), key=lambda s: (s % max(1, half // 2), s))
    return [0] + far + list(range(half - 1, 0, -1))


def forward_kernel(devices, group, waves, pos_ref, spec_ref, basis_ref, trunc_ref, perm_ref, *rest):
    outs, fold = rest[:devices], rest[devices:]
    pos = pos_ref[0]
    levels = outs[0].shape[3] // 4
    half_slots = spec_ref.shape[3]
    tiles = 4 * levels // LANES
    jj = perm_ref.shape[1] // 2
    pairs = jj // devices
    first = pos * waves + pl.program_id(0) * group
    slot = 2 * lax.broadcasted_iota(jnp.int32, (1, half_slots), 1)
    trunc = trunc_ref[...]

    def one(m, carry):
        wave = first + m
        parity = []
        for p in range(2):
            spec = spec_ref[m, p]
            spec = jnp.where(slot + (wave + p) < 2 * half_slots, spec, jnp.zeros_like(spec))
            parity.append(jnp.dot(spec, basis_ref[m, p], preferred_element_type=F32))
        both = jnp.concatenate([parity[0] + parity[1], parity[0] - parity[1]], axis=0)
        both = jnp.where(trunc > wave, both, 0.0).astype(BF16)
        both = jnp.dot(both, perm_ref[...], preferred_element_type=F32)
        for r in range(2):
            rows = []
            for half in range(2):
                for hemi in range(2):
                    at = (2 * hemi + r) * levels
                    rows.append(both[at : at + levels, half * jj : (half + 1) * jj])
            turned = jnp.concatenate(rows, axis=0).T
            for t in range(tiles):
                at = pl.ds(m, jj, stride=group)
                fold[r * tiles + t][at, :] = turned[:, t * LANES : (t + 1) * LANES]
        return carry

    lax.fori_loop(0, group, one, 0)
    size = pairs * group
    for i, s in enumerate(exchange_order(devices)):
        at = pl.multiple_of((pos ^ s) * size, 8)
        for r in range(2):
            for t in range(tiles):
                block = fold[r * tiles + t][pl.ds(at, size), :].reshape(pairs, group, LANES)
                outs[i][:, r, :, t * LANES : (t + 1) * LANES] = block.astype(BF16)


def forward(pos, spec, basis, trunc, perm, devices):
    waves, _, channels, half_slots = spec.shape
    half_lats = basis.shape[3]
    group = min(8, waves)
    pairs = half_lats // (2 * devices)
    lanes = 2 * channels
    return pl.pallas_call(
        functools.partial(forward_kernel, devices, group, waves),
        grid_spec=pltpu.PrefetchScalarGridSpec(
            num_scalar_prefetch=1,
            grid=(waves // group,),
            in_specs=[
                pl.BlockSpec((group, 2, channels, half_slots), lambda i, s: (i, 0, 0, 0)),
                pl.BlockSpec((group, 2, half_slots, half_lats), lambda i, s: (i, 0, 0, 0)),
                pl.BlockSpec((1, half_lats), lambda i, s: (0, 0)),
                pl.BlockSpec((half_lats, half_lats), lambda i, s: (0, 0)),
            ],
            out_specs=[pl.BlockSpec((pairs, 2, group, lanes), lambda i, s: (0, 0, i, 0))] * devices,
            scratch_shapes=[pltpu.VMEM((half_lats // 2 * group, LANES), F32)] * (2 * lanes // LANES),
        ),
        out_shape=[jax.ShapeDtypeStruct((pairs, 2, waves, lanes), BF16)] * devices,
        compiler_params=params(),
        name="forward",
    )(pos, spec, basis, trunc, perm)


def synth_kernel(devices, waves, scale, pos_ref, table_ref, mix_ref, coef_ref, *rest):
    blocks = rest[:devices]
    out_ref, mean_ref, coeffs, tend = rest[devices:]
    pos = pos_ref[0]
    total = devices * waves
    for i, s in enumerate(exchange_order(devices)):
        at = pl.multiple_of((pos ^ s) * waves, 8)
        for r in range(2):
            coeffs[pl.ds(r * total + at, waves), :] = blocks[i][0, r]
    lons = table_ref.shape[0]
    step = lons // 4

    def one(t, total_sum):
        at = pl.multiple_of(t * step, step)
        temp = scale * jnp.dot(
            table_ref[pl.ds(at, step), :], coeffs[...], preferred_element_type=F32
        )
        high = temp.astype(BF16)
        mixed = jnp.dot(high, mix_ref[...], preferred_element_type=F32)
        value = mixed + temp * temp * (coef_ref[0:1, :] - coef_ref[1:2, :] * temp)
        tend[pl.ds(at, step), :] = value
        return total_sum + jnp.sum(value, axis=0, keepdims=True)

    zero = jnp.zeros((1, out_ref.shape[2]), F32)
    mean = lax.fori_loop(0, 4, one, zero) * (1.0 / lons)
    mean_ref[0] = jnp.broadcast_to(mean, mean_ref.shape[1:])

    def two(t, carry):
        at = pl.multiple_of(t * step, step)
        out_ref[0, pl.ds(at, step), :] = (tend[pl.ds(at, step), :] - mean).astype(BF16)
        return carry

    lax.fori_loop(0, 4, two, 0)


def synthesise(pos, table, mix, coef, blocks):
    devices = len(blocks)
    pairs, _, waves, lanes = blocks[0].shape
    lons, depth = table.shape
    return pl.pallas_call(
        functools.partial(synth_kernel, devices, waves, 1.0 / math.sqrt(devices * waves)),
        grid_spec=pltpu.PrefetchScalarGridSpec(
            num_scalar_prefetch=1,
            grid=(pairs,),
            in_specs=[
                pl.BlockSpec((lons, depth), lambda q, s: (0, 0)),
                pl.BlockSpec((lanes, lanes), lambda q, s: (0, 0)),
                pl.BlockSpec((2, lanes), lambda q, s: (0, 0)),
            ]
            + [pl.BlockSpec((1, 2, waves, lanes), lambda q, s: (q, 0, 0, 0))] * devices,
            out_specs=[
                pl.BlockSpec((1, lons, lanes), lambda q, s: (q, 0, 0)),
                pl.BlockSpec((1, 8, lanes), lambda q, s: (q, 0, 0)),
            ],
            scratch_shapes=[pltpu.VMEM((depth, lanes), BF16), pltpu.VMEM((lons, lanes), F32)],
        ),
        out_shape=[
            jax.ShapeDtypeStruct((pairs, lons, lanes), BF16),
            jax.ShapeDtypeStruct((pairs, 8, lanes), F32),
        ],
        compiler_params=params(),
        name="synthesise",
    )(pos, table, mix, coef, *blocks)


def analyse_kernel(devices, waves, scale, pos_ref, table_ref, sums_ref, shifted_ref, excess_ref, *rest):
    outs, full = rest[:devices], rest[devices]
    pos = pos_ref[0]
    total = devices * waves
    depth = table_ref.shape[0]
    step = depth // 4
    excess = excess_ref[0, 0:1, :]

    def one(t, carry):
        at = pl.multiple_of(t * step, step)
        value = jnp.dot(table_ref[pl.ds(at, step), :], shifted_ref[0], preferred_element_type=F32)
        value = value + sums_ref[pl.ds(at, step), :] * excess
        full[pl.ds(at, step), :] = (scale * value).astype(BF16)
        return carry

    lax.fori_loop(0, 4, one, 0)
    for i, s in enumerate(exchange_order(devices)):
        at = pl.multiple_of((pos ^ s) * waves, 8)
        for r in range(2):
            outs[i][0, r] = full[pl.ds(r * total + at, waves), :]


def analyse(pos, table, sums, shifted, excess, devices, waves):
    pairs, lons, lanes = shifted.shape
    depth = table.shape[0]
    return pl.pallas_call(
        functools.partial(analyse_kernel, devices, waves, math.sqrt(2.0 / lons)),
        grid_spec=pltpu.PrefetchScalarGridSpec(
            num_scalar_prefetch=1,
            grid=(pairs,),
            in_specs=[
                pl.BlockSpec((depth, lons), lambda q, s: (0, 0)),
                pl.BlockSpec((depth, 1), lambda q, s: (0, 0)),
                pl.BlockSpec((1, lons, lanes), lambda q, s: (q, 0, 0)),
                pl.BlockSpec((1, 8, lanes), lambda q, s: (q, 0, 0)),
            ],
            out_specs=[pl.BlockSpec((1, 2, waves, lanes), lambda q, s: (q, 0, 0, 0))] * devices,
            scratch_shapes=[pltpu.VMEM((depth, lanes), BF16)],
        ),
        out_shape=[jax.ShapeDtypeStruct((pairs, 2, waves, lanes), BF16)] * devices,
        compiler_params=params(),
        name="analyse",
    )(pos, table, sums, shifted, excess)


def inverse_kernel(devices, group, waves, pos_ref, spec_ref, basis_ref, trunc_ref, weight_ref, perm_ref, *rest):
    blocks = rest[:devices]
    out_ref, fold = rest[devices], rest[devices + 1 :]
    pos = pos_ref[0]
    levels = blocks[0].shape[3] // 4
    half_slots = spec_ref.shape[3]
    jj = perm_ref.shape[0] // 2
    pairs = jj // devices
    tiles = 4 * levels // LANES
    size = pairs * group
    for i, s in enumerate(exchange_order(devices)):
        at = pl.multiple_of((pos ^ s) * size, 8)
        for r in range(2):
            for t in range(tiles):
                block = blocks[i][:, r, :, t * LANES : (t + 1) * LANES].astype(F32)
                fold[r * tiles + t][pl.ds(at, size), :] = block.reshape(size, LANES)
    first = pos * waves + pl.program_id(0) * group
    slot = 2 * lax.broadcasted_iota(jnp.int32, (1, half_slots), 1)
    trunc = trunc_ref[...]
    weight = weight_ref[...]

    def one(m, carry):
        wave = first + m
        turned = []
        for r in range(2):
            at = pl.ds(m, jj, stride=group)
            columns = [fold[r * tiles + t][at, :].T for t in range(tiles)]
            turned.append(jnp.concatenate(columns, axis=0))
        rows = []
        for hemi in range(2):
            for r in range(2):
                pieces = []
                for half in range(2):
                    at = (2 * half + hemi) * levels
                    pieces.append(turned[r][at : at + levels])
                rows.append(jnp.concatenate(pieces, axis=1))
        both = jnp.concatenate(rows, axis=0).astype(BF16)
        both = jnp.dot(both, perm_ref[...], preferred_element_type=F32)
        both = jnp.where(trunc > wave, both, 0.0)
        channels = 2 * levels
        north, south = both[:channels], both[channels:]
        for p in range(2):
            folded = (weight * (north + south if p == 0 else north - south)).astype(BF16)
            direct = lax.dot_general(
                folded, basis_ref[m, p], (((1,), (1,)), ((), ())), preferred_element_type=F32
            )
            value = spec_ref[m, p].astype(F32) + direct
            out_ref[m, p] = jnp.where(slot + (wave + p) < 2 * half_slots, value, 0.0).astype(BF16)
        return carry

    lax.fori_loop(0, group, one, 0)


def inverse(pos, spec, basis, trunc, weight, perm, blocks):
    devices = len(blocks)
    waves, _, channels, half_slots = spec.shape
    half_lats = basis.shape[3]
    group = min(8, waves)
    pairs = half_lats // (2 * devices)
    lanes = 2 * channels
    return pl.pallas_call(
        functools.partial(inverse_kernel, devices, group, waves),
        grid_spec=pltpu.PrefetchScalarGridSpec(
            num_scalar_prefetch=1,
            grid=(waves // group,),
            in_specs=[
                pl.BlockSpec((group, 2, channels, half_slots), lambda i, s: (i, 0, 0, 0)),
                pl.BlockSpec((group, 2, half_slots, half_lats), lambda i, s: (i, 0, 0, 0)),
                pl.BlockSpec((1, half_lats), lambda i, s: (0, 0)),
                pl.BlockSpec((1, half_lats), lambda i, s: (0, 0)),
                pl.BlockSpec((half_lats, half_lats), lambda i, s: (0, 0)),
            ]
            + [pl.BlockSpec((pairs, 2, group, lanes), lambda i, s: (0, 0, i, 0))] * devices,
            out_specs=pl.BlockSpec((group, 2, channels, half_slots), lambda i, s: (i, 0, 0, 0)),
            scratch_shapes=[pltpu.VMEM((half_lats // 2 * group, LANES), F32)] * (2 * lanes // LANES),
        ),
        out_shape=jax.ShapeDtypeStruct(spec.shape, BF16),
        compiler_params=params(),
        name="inverse",
    )(pos, spec, basis, trunc, weight, perm, *blocks)


def cos_sin(rows, columns):
    phases = rows[:, None] * columns[None, :] % NLON
    angles = phases.astype(F32) * (2.0 * math.pi / NLON)
    return jnp.cos(angles), jnp.sin(angles)


def fourier_tables(waves, lons):
    def outer(rows, columns):
        low = 32
        col = jnp.arange(columns, dtype=jnp.int32)
        small = lax.optimization_barrier(
            cos_sin(jnp.arange(low, dtype=jnp.int32), col)
            + cos_sin(low * jnp.arange(rows // low, dtype=jnp.int32), col)
        )
        c0, s0, c1, s1 = small
        cos = c1[:, None] * c0[None] - s1[:, None] * s0[None]
        sin = s1[:, None] * c0[None] + c1[:, None] * s0[None]
        return cos.reshape(rows, columns).astype(BF16), (-sin).reshape(rows, columns).astype(BF16)

    analysis = jnp.concatenate(outer(waves, lons), axis=0)
    synthesis = jnp.concatenate(outer(lons, waves), axis=1)
    return synthesis, analysis


def exchange(arrays, devices, needed):
    got = [arrays[0]]
    for array, s in list(zip(arrays, exchange_order(devices)))[1:]:
        pairs = [(i, i ^ s) for i in range(devices) if needed(i, i ^ s)]
        got.append(lax.ppermute(array, "wave", pairs))
    return got


def sum_over_wave(value, devices):
    span = 1
    while span < devices:
        others = [k * span for k in range(1, 4) if k * span < devices]
        moved = [
            lax.ppermute(value, "wave", [(i, i ^ k) for i in range(devices)]) for k in others
        ]
        for part in moved:
            value = value + part
        span *= 4
    return value


def per_device(spectral, basis, quad_weights, column, square_coef, cube_coef, trunc):
    devices = lax.axis_size("wave")
    position = lax.axis_index("wave").astype(jnp.int32)
    waves, _, half_slots, channels = spectral.shape
    half_lats = basis.shape[3]
    levels = channels // 2
    rows = half_lats // devices
    pairs = rows // 2
    pos = position.reshape(1)
    spec = jnp.swapaxes(spectral, 2, 3)
    order = latitude_order(half_lats, devices)
    lats = jnp.arange(half_lats, dtype=jnp.int32)
    perm = (lats[:, None] == order[None, :]).astype(BF16)
    back = (order[:, None] == lats[None, :]).astype(BF16)
    trunc_row = trunc.reshape(1, half_lats)
    weight_row = quad_weights.reshape(1, half_lats)
    blocks = forward(pos, spec, basis, trunc_row, perm, devices)

    reach = [min(devices, g + 1 + max(1, devices // 16)) for g in range(devices)]
    top = jnp.max(trunc.reshape(devices, rows), axis=1)
    fits = jnp.all(top <= waves * jnp.array(reach, dtype=jnp.int32))

    def finish(sparse, blocks):
        def there(source, owner):
            return not sparse or source < reach[devices - 1 - owner]

        def home(owner, source):
            return there(source, owner)

        synthesis, analysis = fourier_tables(devices * waves, NLON)
        sums = jnp.sum(analysis.astype(F32), axis=1, keepdims=True)
        mix = jnp.kron(jnp.eye(4, dtype=F32), column.T).astype(BF16)
        coef = jnp.stack([jnp.tile(square_coef, 4), jnp.tile(cube_coef, 4)])
        group = devices - 1 - position
        own = lax.dynamic_slice(quad_weights, (group * rows,), (rows,)).reshape(2, pairs)
        own = own.T[:, :, None, None]
        norm = 1.0 / (2.0 * jnp.sum(quad_weights))

        got = exchange(blocks, devices, there)
        shifted, means = synthesise(pos, synthesis, mix, coef, got)
        zonal = means[:, 0].reshape(pairs, 2, 2, levels)
        level_mean = sum_over_wave(jnp.sum(own * zonal, axis=(0, 1, 2)), devices) * norm
        excess = means - jnp.tile(level_mean, 4)
        parts = analyse(pos, analysis, sums, shifted, excess, devices, waves)
        parts = exchange(parts, devices, home)
        return inverse(pos, spec, basis, trunc_row, weight_row, back, parts)

    out = lax.cond(
        fits, functools.partial(finish, True), functools.partial(finish, False), blocks
    )
    return jnp.swapaxes(out, 2, 3)


def solution(mesh):
    return jax.shard_map(
        per_device,
        mesh=mesh,
        in_specs=(
            P(("member", "wave"), None, None, None),
            P("wave", None, None, None),
            P(),
            P(),
            P(),
            P(),
            P(),
        ),
        out_specs=P(("member", "wave"), None, None, None),
        check_vma=False,
    )
```

```python
import functools
import math

import jax
import jax.numpy as jnp
from jax import lax
from jax.experimental import pallas as pl
from jax.experimental.pallas import tpu as pltpu
from jax.sharding import PartitionSpec as P

NLON = 1024
LANES = 128
F32 = jnp.float32
BF16 = jnp.bfloat16
STEPS = 4
UNROLL = 4
VMEM_LIMIT = 56 * 1024 * 1024


def params():
    return pltpu.CompilerParams(
        dimension_semantics=("arbitrary",), vmem_limit_bytes=VMEM_LIMIT
    )


def latitude_order(half_lats, devices):
    rows = half_lats // devices
    pairs = rows // 2
    lane = jnp.arange(half_lats, dtype=jnp.int32)
    half = lane // (half_lats // 2)
    owner = lane % (half_lats // 2) // pairs
    pair = lane % pairs
    return (devices - 1 - owner) * rows + half * pairs + pair


def exchange_order(devices):
    quarter = max(1, devices // 4)
    order = [0]
    for t in range(quarter):
        order += [quarter + t, 3 * quarter + t]
    order += [2 * quarter + t for t in range(quarter)]
    return order + list(range(quarter - 1, 0, -1))


def forward_kernel(devices, group, waves, pos_ref, spec_ref, basis_ref, trunc_ref, perm_ref, *rest):
    outs, fold = rest[:devices], rest[devices:]
    pos = pos_ref[0]
    levels = outs[0].shape[3] // 4
    half_slots = spec_ref.shape[3]
    tiles = 4 * levels // LANES
    jj = perm_ref.shape[1] // 2
    pairs = jj // devices
    first = pos * waves + pl.program_id(0) * group
    slot = 2 * lax.broadcasted_iota(jnp.int32, (1, half_slots), 1)
    trunc = trunc_ref[...]

    def one(m, carry):
        wave = first + m
        parity = []
        for p in range(2):
            spec = spec_ref[m, p]
            spec = jnp.where(slot + (wave + p) < 2 * half_slots, spec, jnp.zeros_like(spec))
            parity.append(jnp.dot(spec, basis_ref[m, p], preferred_element_type=F32))
        both = jnp.concatenate([parity[0] + parity[1], parity[0] - parity[1]], axis=0)
        both = jnp.where(trunc > wave, both, 0.0).astype(BF16)
        both = jnp.dot(both, perm_ref[...], preferred_element_type=F32)
        for r in range(2):
            rows = []
            for half in range(2):
                for hemi in range(2):
                    at = (2 * hemi + r) * levels
                    rows.append(both[at : at + levels, half * jj : (half + 1) * jj])
            turned = jnp.concatenate(rows, axis=0).T
            for t in range(tiles):
                at = pl.ds(m, jj, stride=group)
                fold[r * tiles + t][at, :] = turned[:, t * LANES : (t + 1) * LANES]
        return carry

    lax.fori_loop(0, group, one, 0, unroll=group)
    size = pairs * group
    for i, s in enumerate(exchange_order(devices)):
        at = pl.multiple_of((pos ^ s) * size, 8)
        for r in range(2):
            for t in range(tiles):
                block = fold[r * tiles + t][pl.ds(at, size), :].reshape(pairs, group, LANES)
                outs[i][:, r, :, t * LANES : (t + 1) * LANES] = block.astype(BF16)


def forward(pos, spec, basis, trunc, perm, devices):
    waves, _, channels, half_slots = spec.shape
    half_lats = basis.shape[3]
    group = min(8, waves)
    pairs = half_lats // (2 * devices)
    lanes = 2 * channels
    return pl.pallas_call(
        functools.partial(forward_kernel, devices, group, waves),
        grid_spec=pltpu.PrefetchScalarGridSpec(
            num_scalar_prefetch=1,
            grid=(waves // group,),
            in_specs=[
                pl.BlockSpec((group, 2, channels, half_slots), lambda i, s: (i, 0, 0, 0)),
                pl.BlockSpec((group, 2, half_slots, half_lats), lambda i, s: (i, 0, 0, 0)),
                pl.BlockSpec((1, half_lats), lambda i, s: (0, 0)),
                pl.BlockSpec((half_lats, half_lats), lambda i, s: (0, 0)),
            ],
            out_specs=[pl.BlockSpec((pairs, 2, group, lanes), lambda i, s: (0, 0, i, 0))] * devices,
            scratch_shapes=[pltpu.VMEM((half_lats // 2 * group, LANES), F32)] * (2 * lanes // LANES),
        ),
        out_shape=[jax.ShapeDtypeStruct((pairs, 2, waves, lanes), BF16)] * devices,
        compiler_params=params(),
        name="forward",
    )(pos, spec, basis, trunc, perm)


def synth_kernel(devices, waves, scale, pos_ref, table_ref, mix_ref, coef_ref, *rest):
    blocks = rest[:devices]
    out_ref, mean_ref, coeffs, tend = rest[devices:]
    pos = pos_ref[0]
    total = devices * waves
    count, lanes = blocks[0].shape[0], blocks[0].shape[3]
    for i, s in enumerate(exchange_order(devices)):
        at = pl.multiple_of((pos ^ s) * waves, 8)
        for r in range(2):
            for c in range(count):
                part = blocks[i][c, r]
                coeffs[pl.ds(r * total + at, waves), c * lanes : (c + 1) * lanes] = part
    lons = table_ref.shape[0]
    step = lons // STEPS

    def one(t, total_sum):
        at = pl.multiple_of(t * step, step)
        temp = scale * jnp.dot(
            table_ref[pl.ds(at, step), :], coeffs[...], preferred_element_type=F32
        )
        sums = []
        for c in range(count):
            mine = temp[:, c * lanes : (c + 1) * lanes]
            mixed = jnp.dot(mine.astype(BF16), mix_ref[...], preferred_element_type=F32)
            value = mixed + mine * mine * (coef_ref[0:1, :] - coef_ref[1:2, :] * mine)
            tend[pl.ds(at, step), c * lanes : (c + 1) * lanes] = value
            sums.append(jnp.sum(value, axis=0, keepdims=True))
        return total_sum + jnp.concatenate(sums, axis=1)

    zero = jnp.zeros((1, out_ref.shape[2]), F32)
    mean = lax.fori_loop(0, STEPS, one, zero, unroll=UNROLL) * (1.0 / lons)
    mean_ref[0] = jnp.broadcast_to(mean, mean_ref.shape[1:])

    def two(t, carry):
        at = pl.multiple_of(t * step, step)
        out_ref[0, pl.ds(at, step), :] = (tend[pl.ds(at, step), :] - mean).astype(BF16)
        return carry

    lax.fori_loop(0, STEPS, two, 0)


def synthesise(pos, table, mix, coef, blocks):
    devices = len(blocks)
    pairs, _, waves, lanes = blocks[0].shape
    lons, depth = table.shape
    count = 2 if pairs % 2 == 0 else 1
    width = count * lanes
    return pl.pallas_call(
        functools.partial(synth_kernel, devices, waves, 1.0 / math.sqrt(devices * waves)),
        grid_spec=pltpu.PrefetchScalarGridSpec(
            num_scalar_prefetch=1,
            grid=(pairs // count,),
            in_specs=[
                pl.BlockSpec((lons, depth), lambda q, s: (0, 0)),
                pl.BlockSpec((lanes, lanes), lambda q, s: (0, 0)),
                pl.BlockSpec((2, lanes), lambda q, s: (0, 0)),
            ]
            + [pl.BlockSpec((count, 2, waves, lanes), lambda q, s: (q, 0, 0, 0))] * devices,
            out_specs=[
                pl.BlockSpec((1, lons, width), lambda q, s: (q, 0, 0)),
                pl.BlockSpec((1, 8, width), lambda q, s: (q, 0, 0)),
            ],
            scratch_shapes=[pltpu.VMEM((depth, width), BF16), pltpu.VMEM((lons, width), F32)],
        ),
        out_shape=[
            jax.ShapeDtypeStruct((pairs // count, lons, width), BF16),
            jax.ShapeDtypeStruct((pairs // count, 8, width), F32),
        ],
        compiler_params=params(),
        name="synthesise",
    )(pos, table, mix, coef, *blocks)


def analyse_kernel(devices, waves, scale, pos_ref, table_ref, sums_ref, shifted_ref, excess_ref, *rest):
    outs, full = rest[:devices], rest[devices]
    pos = pos_ref[0]
    total = devices * waves
    depth = table_ref.shape[0]
    count, lanes = outs[0].shape[0], outs[0].shape[3]
    step = depth // STEPS
    excess = excess_ref[0, 0:1, :]

    def one(t, carry):
        at = pl.multiple_of(t * step, step)
        value = jnp.dot(table_ref[pl.ds(at, step), :], shifted_ref[0], preferred_element_type=F32)
        value = value + sums_ref[pl.ds(at, step), :] * excess
        full[pl.ds(at, step), :] = (scale * value).astype(BF16)
        return carry

    lax.fori_loop(0, STEPS, one, 0, unroll=UNROLL)
    for i, s in enumerate(exchange_order(devices)):
        at = pl.multiple_of((pos ^ s) * waves, 8)
        for r in range(2):
            for c in range(count):
                part = full[pl.ds(r * total + at, waves), c * lanes : (c + 1) * lanes]
                outs[i][c, r] = part


def analyse(pos, table, sums, shifted, excess, devices, waves, count):
    steps, lons, width = shifted.shape
    lanes = width // count
    depth = table.shape[0]
    return pl.pallas_call(
        functools.partial(analyse_kernel, devices, waves, math.sqrt(2.0 / lons)),
        grid_spec=pltpu.PrefetchScalarGridSpec(
            num_scalar_prefetch=1,
            grid=(steps,),
            in_specs=[
                pl.BlockSpec((depth, lons), lambda q, s: (0, 0)),
                pl.BlockSpec((depth, 1), lambda q, s: (0, 0)),
                pl.BlockSpec((1, lons, width), lambda q, s: (q, 0, 0)),
                pl.BlockSpec((1, 8, width), lambda q, s: (q, 0, 0)),
            ],
            out_specs=[pl.BlockSpec((count, 2, waves, lanes), lambda q, s: (q, 0, 0, 0))] * devices,
            scratch_shapes=[pltpu.VMEM((depth, width), BF16)],
        ),
        out_shape=[jax.ShapeDtypeStruct((steps * count, 2, waves, lanes), BF16)] * devices,
        compiler_params=params(),
        name="analyse",
    )(pos, table, sums, shifted, excess)


def inverse_kernel(devices, group, waves, pos_ref, spec_ref, basis_ref, trunc_ref, weight_ref, perm_ref, *rest):
    blocks = rest[:devices]
    out_ref, fold = rest[devices], rest[devices + 1 :]
    pos = pos_ref[0]
    levels = blocks[0].shape[3] // 4
    half_slots = spec_ref.shape[3]
    jj = perm_ref.shape[0] // 2
    pairs = jj // devices
    tiles = 4 * levels // LANES
    size = pairs * group
    for i, s in enumerate(exchange_order(devices)):
        at = pl.multiple_of((pos ^ s) * size, 8)
        for r in range(2):
            for t in range(tiles):
                block = blocks[i][:, r, :, t * LANES : (t + 1) * LANES].astype(F32)
                fold[r * tiles + t][pl.ds(at, size), :] = block.reshape(size, LANES)
    first = pos * waves + pl.program_id(0) * group
    slot = 2 * lax.broadcasted_iota(jnp.int32, (1, half_slots), 1)
    trunc = trunc_ref[...]
    weight = weight_ref[...]

    def one(m, carry):
        wave = first + m
        turned = []
        for r in range(2):
            at = pl.ds(m, jj, stride=group)
            columns = [fold[r * tiles + t][at, :].T for t in range(tiles)]
            turned.append(jnp.concatenate(columns, axis=0))
        rows = []
        for hemi in range(2):
            for r in range(2):
                pieces = []
                for half in range(2):
                    at = (2 * half + hemi) * levels
                    pieces.append(turned[r][at : at + levels])
                rows.append(jnp.concatenate(pieces, axis=1))
        both = jnp.concatenate(rows, axis=0).astype(BF16)
        both = jnp.dot(both, perm_ref[...], preferred_element_type=F32)
        both = jnp.where(trunc > wave, both, 0.0)
        channels = 2 * levels
        north, south = both[:channels], both[channels:]
        for p in range(2):
            folded = (weight * (north + south if p == 0 else north - south)).astype(BF16)
            direct = lax.dot_general(
                folded, basis_ref[m, p], (((1,), (1,)), ((), ())), preferred_element_type=F32
            )
            value = spec_ref[m, p].astype(F32) + direct
            out_ref[m, p] = jnp.where(slot + (wave + p) < 2 * half_slots, value, 0.0).astype(BF16)
        return carry

    lax.fori_loop(0, group, one, 0, unroll=group)


def inverse(pos, spec, basis, trunc, weight, perm, blocks):
    devices = len(blocks)
    waves, _, channels, half_slots = spec.shape
    half_lats = basis.shape[3]
    group = min(8, waves)
    pairs = half_lats // (2 * devices)
    lanes = 2 * channels
    return pl.pallas_call(
        functools.partial(inverse_kernel, devices, group, waves),
        grid_spec=pltpu.PrefetchScalarGridSpec(
            num_scalar_prefetch=1,
            grid=(waves // group,),
            in_specs=[
                pl.BlockSpec((group, 2, channels, half_slots), lambda i, s: (i, 0, 0, 0)),
                pl.BlockSpec((group, 2, half_slots, half_lats), lambda i, s: (i, 0, 0, 0)),
                pl.BlockSpec((1, half_lats), lambda i, s: (0, 0)),
                pl.BlockSpec((1, half_lats), lambda i, s: (0, 0)),
                pl.BlockSpec((half_lats, half_lats), lambda i, s: (0, 0)),
            ]
            + [pl.BlockSpec((pairs, 2, group, lanes), lambda i, s: (0, 0, i, 0))] * devices,
            out_specs=pl.BlockSpec((group, 2, channels, half_slots), lambda i, s: (i, 0, 0, 0)),
            scratch_shapes=[pltpu.VMEM((half_lats // 2 * group, LANES), F32)] * (2 * lanes // LANES),
        ),
        out_shape=jax.ShapeDtypeStruct(spec.shape, BF16),
        compiler_params=params(),
        name="inverse",
    )(pos, spec, basis, trunc, weight, perm, *blocks)


def cos_sin(rows, columns):
    phases = rows[:, None] * columns[None, :] % NLON
    angles = phases.astype(F32) * (2.0 * math.pi / NLON)
    return jnp.cos(angles), jnp.sin(angles)


def fourier_tables(waves, lons):
    def outer(rows, columns):
        low = 32
        col = jnp.arange(columns, dtype=jnp.int32)
        small = lax.optimization_barrier(
            cos_sin(jnp.arange(low, dtype=jnp.int32), col)
            + cos_sin(low * jnp.arange(rows // low, dtype=jnp.int32), col)
        )
        c0, s0, c1, s1 = small
        cos = c1[:, None] * c0[None] - s1[:, None] * s0[None]
        sin = s1[:, None] * c0[None] + c1[:, None] * s0[None]
        return cos.reshape(rows, columns).astype(BF16), (-sin).reshape(rows, columns).astype(BF16)

    analysis = jnp.concatenate(outer(waves, lons), axis=0)
    synthesis = jnp.concatenate(outer(lons, waves), axis=1)
    return synthesis, analysis


def exchange(arrays, devices, needed):
    got = [arrays[0]]
    for array, s in list(zip(arrays, exchange_order(devices)))[1:]:
        pairs = [(i, i ^ s) for i in range(devices) if needed(i, i ^ s)]
        got.append(lax.ppermute(array, "wave", pairs))
    return got


def sum_over_wave(value, devices):
    span = 1
    while span < devices:
        others = [k * span for k in range(1, 4) if k * span < devices]
        moved = [
            lax.ppermute(value, "wave", [(i, i ^ k) for i in range(devices)]) for k in others
        ]
        for part in moved:
            value = value + part
        span *= 4
    return value


def per_device(spectral, basis, quad_weights, column, square_coef, cube_coef, trunc):
    devices = lax.axis_size("wave")
    position = lax.axis_index("wave").astype(jnp.int32)
    waves, _, half_slots, channels = spectral.shape
    half_lats = basis.shape[3]
    levels = channels // 2
    rows = half_lats // devices
    pairs = rows // 2
    pos = position.reshape(1)
    spec = jnp.swapaxes(spectral, 2, 3)
    order = latitude_order(half_lats, devices)
    lats = jnp.arange(half_lats, dtype=jnp.int32)
    perm = (lats[:, None] == order[None, :]).astype(BF16)
    back = (order[:, None] == lats[None, :]).astype(BF16)
    trunc_row = trunc.reshape(1, half_lats)
    weight_row = quad_weights.reshape(1, half_lats)
    blocks = forward(pos, spec, basis, trunc_row, perm, devices)

    reach = [min(devices, g + 1 + max(1, devices // 16)) for g in range(devices)]
    top = jnp.max(trunc.reshape(devices, rows), axis=1)
    fits = jnp.all(top <= waves * jnp.array(reach, dtype=jnp.int32))

    def finish(sparse, blocks):
        def there(source, owner):
            return not sparse or source < reach[devices - 1 - owner]

        def home(owner, source):
            return there(source, owner)

        synthesis, analysis = fourier_tables(devices * waves, NLON)
        sums = jnp.sum(analysis.astype(F32), axis=1, keepdims=True)
        mix = jnp.kron(jnp.eye(4, dtype=F32), column.T).astype(BF16)
        coef = jnp.stack([jnp.tile(square_coef, 4), jnp.tile(cube_coef, 4)])
        group = devices - 1 - position
        own = lax.dynamic_slice(quad_weights, (group * rows,), (rows,)).reshape(2, pairs)
        own = own.T[:, :, None, None]
        norm = 1.0 / (2.0 * jnp.sum(quad_weights))

        got = exchange(blocks, devices, there)
        shifted, means = synthesise(pos, synthesis, mix, coef, got)
        count = pairs // means.shape[0]
        zonal = means[:, 0].reshape(pairs, 2, 2, levels)
        level_mean = sum_over_wave(jnp.sum(own * zonal, axis=(0, 1, 2)), devices) * norm
        excess = means - jnp.tile(level_mean, 4 * count)
        parts = analyse(pos, analysis, sums, shifted, excess, devices, waves, count)
        parts = exchange(parts, devices, home)
        return inverse(pos, spec, basis, trunc_row, weight_row, back, parts)

    out = lax.cond(
        fits, functools.partial(finish, True), functools.partial(finish, False), blocks
    )
    return jnp.swapaxes(out, 2, 3)


def solution(mesh):
    return jax.shard_map(
        per_device,
        mesh=mesh,
        in_specs=(
            P(("member", "wave"), None, None, None),
            P("wave", None, None, None),
            P(),
            P(),
            P(),
            P(),
            P(),
        ),
        out_specs=P(("member", "wave"), None, None, None),
        check_vma=False,
    )
```

```python
import functools
import math

import jax
import jax.numpy as jnp
from jax import lax
from jax.experimental import pallas as pl
from jax.experimental.pallas import tpu as pltpu
from jax.sharding import PartitionSpec as P

NLON = 1024
LANES = 128
F32 = jnp.float32
BF16 = jnp.bfloat16
STEPS = 4
VMEM_LIMIT = 56 * 1024 * 1024


def params():
    return pltpu.CompilerParams(
        dimension_semantics=("arbitrary",), vmem_limit_bytes=VMEM_LIMIT
    )


def latitude_order(half_lats, devices):
    rows = half_lats // devices
    pairs = rows // 2
    lane = jnp.arange(half_lats, dtype=jnp.int32)
    half = lane // (half_lats // 2)
    owner = lane % (half_lats // 2) // pairs
    pair = lane % pairs
    return (devices - 1 - owner) * rows + half * pairs + pair


def exchange_order(devices):
    quarter = max(1, devices // 4)
    order = [0]
    for part in (1, 3, 2):
        order += [part * quarter + t for t in range(quarter)]
    return order + list(range(quarter - 1, 0, -1))


def forward_kernel(devices, group, waves, pos_ref, spec_ref, basis_ref, trunc_ref, perm_ref, *rest):
    outs, fold = rest[:devices], rest[devices:]
    pos = pos_ref[0]
    levels = outs[0].shape[3] // 4
    half_slots = spec_ref.shape[3]
    tiles = 4 * levels // LANES
    jj = perm_ref.shape[1] // 2
    pairs = jj // devices
    first = pos * waves + pl.program_id(0) * group
    slot = 2 * lax.broadcasted_iota(jnp.int32, (1, half_slots), 1)
    trunc = trunc_ref[...]

    def one(m, carry):
        wave = first + m
        parity = []
        for p in range(2):
            spec = spec_ref[m, p]
            spec = jnp.where(slot + (wave + p) < 2 * half_slots, spec, jnp.zeros_like(spec))
            parity.append(jnp.dot(spec, basis_ref[m, p], preferred_element_type=F32))
        both = jnp.concatenate([parity[0] + parity[1], parity[0] - parity[1]], axis=0)
        both = jnp.where(trunc > wave, both, 0.0).astype(BF16)
        both = jnp.dot(both, perm_ref[...], preferred_element_type=F32)
        for r in range(2):
            rows = []
            for half in range(2):
                for hemi in range(2):
                    at = (2 * hemi + r) * levels
                    rows.append(both[at : at + levels, half * jj : (half + 1) * jj])
            turned = jnp.concatenate(rows, axis=0).T
            for t in range(tiles):
                at = pl.ds(m, jj, stride=group)
                fold[r * tiles + t][at, :] = turned[:, t * LANES : (t + 1) * LANES]
        return carry

    lax.fori_loop(0, group, one, 0, unroll=group)
    size = pairs * group
    for i, s in enumerate(exchange_order(devices)):
        at = pl.multiple_of((pos ^ s) * size, 8)
        for r in range(2):
            for t in range(tiles):
                block = fold[r * tiles + t][pl.ds(at, size), :].reshape(pairs, group, LANES)
                outs[i][:, r, :, t * LANES : (t + 1) * LANES] = block.astype(BF16)


def forward(pos, spec, basis, trunc, perm, devices):
    waves, _, channels, half_slots = spec.shape
    half_lats = basis.shape[3]
    group = min(8, waves)
    pairs = half_lats // (2 * devices)
    lanes = 2 * channels
    return pl.pallas_call(
        functools.partial(forward_kernel, devices, group, waves),
        grid_spec=pltpu.PrefetchScalarGridSpec(
            num_scalar_prefetch=1,
            grid=(waves // group,),
            in_specs=[
                pl.BlockSpec((group, 2, channels, half_slots), lambda i, s: (i, 0, 0, 0)),
                pl.BlockSpec((group, 2, half_slots, half_lats), lambda i, s: (i, 0, 0, 0)),
                pl.BlockSpec((1, half_lats), lambda i, s: (0, 0)),
                pl.BlockSpec((half_lats, half_lats), lambda i, s: (0, 0)),
            ],
            out_specs=[pl.BlockSpec((pairs, 2, group, lanes), lambda i, s: (0, 0, i, 0))] * devices,
            scratch_shapes=[pltpu.VMEM((half_lats // 2 * group, LANES), F32)] * (2 * lanes // LANES),
        ),
        out_shape=[jax.ShapeDtypeStruct((pairs, 2, waves, lanes), BF16)] * devices,
        compiler_params=params(),
        name="forward",
    )(pos, spec, basis, trunc, perm)


def synth_kernel(devices, waves, unroll, scale, pos_ref, table_ref, mix_ref, coef_ref, *rest):
    blocks = rest[:devices]
    out_ref, mean_ref, coeffs, tend = rest[devices:]
    pos = pos_ref[0]
    total = devices * waves
    count, lanes = blocks[0].shape[0], blocks[0].shape[3]
    for i, s in enumerate(exchange_order(devices)):
        at = pl.multiple_of((pos ^ s) * waves, 8)
        for r in range(2):
            for c in range(count):
                part = blocks[i][c, r]
                coeffs[pl.ds(r * total + at, waves), c * lanes : (c + 1) * lanes] = part
    lons = table_ref.shape[0]
    step = lons // STEPS

    def one(t, total_sum):
        at = pl.multiple_of(t * step, step)
        temp = scale * jnp.dot(
            table_ref[pl.ds(at, step), :], coeffs[...], preferred_element_type=F32
        )
        sums = []
        for c in range(count):
            mine = temp[:, c * lanes : (c + 1) * lanes]
            mixed = jnp.dot(mine.astype(BF16), mix_ref[...], preferred_element_type=F32)
            value = mixed + mine * mine * (coef_ref[0:1, :] - coef_ref[1:2, :] * mine)
            tend[pl.ds(at, step), c * lanes : (c + 1) * lanes] = value
            sums.append(jnp.sum(value, axis=0, keepdims=True))
        return total_sum + jnp.concatenate(sums, axis=1)

    zero = jnp.zeros((1, out_ref.shape[2]), F32)
    mean = lax.fori_loop(0, STEPS, one, zero, unroll=unroll) * (1.0 / lons)
    mean_ref[0] = jnp.broadcast_to(mean, mean_ref.shape[1:])

    def two(t, carry):
        at = pl.multiple_of(t * step, step)
        out_ref[0, pl.ds(at, step), :] = (tend[pl.ds(at, step), :] - mean).astype(BF16)
        return carry

    lax.fori_loop(0, STEPS, two, 0)


def synthesise(pos, table, mix, coef, blocks, unroll):
    devices = len(blocks)
    pairs, _, waves, lanes = blocks[0].shape
    lons, depth = table.shape
    count = 2 if pairs % 2 == 0 else 1
    width = count * lanes
    return pl.pallas_call(
        functools.partial(synth_kernel, devices, waves, unroll, 1.0 / math.sqrt(devices * waves)),
        grid_spec=pltpu.PrefetchScalarGridSpec(
            num_scalar_prefetch=1,
            grid=(pairs // count,),
            in_specs=[
                pl.BlockSpec((lons, depth), lambda q, s: (0, 0)),
                pl.BlockSpec((lanes, lanes), lambda q, s: (0, 0)),
                pl.BlockSpec((2, lanes), lambda q, s: (0, 0)),
            ]
            + [pl.BlockSpec((count, 2, waves, lanes), lambda q, s: (q, 0, 0, 0))] * devices,
            out_specs=[
                pl.BlockSpec((1, lons, width), lambda q, s: (q, 0, 0)),
                pl.BlockSpec((1, 8, width), lambda q, s: (q, 0, 0)),
            ],
            scratch_shapes=[pltpu.VMEM((depth, width), BF16), pltpu.VMEM((lons, width), F32)],
        ),
        out_shape=[
            jax.ShapeDtypeStruct((pairs // count, lons, width), BF16),
            jax.ShapeDtypeStruct((pairs // count, 8, width), F32),
        ],
        compiler_params=params(),
        name="synthesise",
    )(pos, table, mix, coef, *blocks)


def analyse_kernel(devices, waves, unroll, scale, pos_ref, table_ref, sums_ref, shifted_ref, excess_ref, *rest):
    outs, full = rest[:devices], rest[devices]
    pos = pos_ref[0]
    total = devices * waves
    depth = table_ref.shape[0]
    count, lanes = outs[0].shape[0], outs[0].shape[3]
    step = depth // STEPS
    excess = excess_ref[0, 0:1, :]

    def one(t, carry):
        at = pl.multiple_of(t * step, step)
        value = jnp.dot(table_ref[pl.ds(at, step), :], shifted_ref[0], preferred_element_type=F32)
        value = value + sums_ref[pl.ds(at, step), :] * excess
        full[pl.ds(at, step), :] = (scale * value).astype(BF16)
        return carry

    lax.fori_loop(0, STEPS, one, 0, unroll=unroll)
    for i, s in enumerate(exchange_order(devices)):
        at = pl.multiple_of((pos ^ s) * waves, 8)
        for r in range(2):
            for c in range(count):
                part = full[pl.ds(r * total + at, waves), c * lanes : (c + 1) * lanes]
                outs[i][c, r] = part


def analyse(pos, table, sums, shifted, excess, devices, waves, count, unroll):
    steps, lons, width = shifted.shape
    lanes = width // count
    depth = table.shape[0]
    return pl.pallas_call(
        functools.partial(analyse_kernel, devices, waves, unroll, math.sqrt(2.0 / lons)),
        grid_spec=pltpu.PrefetchScalarGridSpec(
            num_scalar_prefetch=1,
            grid=(steps,),
            in_specs=[
                pl.BlockSpec((depth, lons), lambda q, s: (0, 0)),
                pl.BlockSpec((depth, 1), lambda q, s: (0, 0)),
                pl.BlockSpec((1, lons, width), lambda q, s: (q, 0, 0)),
                pl.BlockSpec((1, 8, width), lambda q, s: (q, 0, 0)),
            ],
            out_specs=[pl.BlockSpec((count, 2, waves, lanes), lambda q, s: (q, 0, 0, 0))] * devices,
            scratch_shapes=[pltpu.VMEM((depth, width), BF16)],
        ),
        out_shape=[jax.ShapeDtypeStruct((steps * count, 2, waves, lanes), BF16)] * devices,
        compiler_params=params(),
        name="analyse",
    )(pos, table, sums, shifted, excess)


def inverse_kernel(
    devices, group, waves, unroll, pos_ref, sums_ref, spec_ref, basis_ref, trunc_ref, weight_ref, perm_ref,
    share_ref, *rest
):
    blocks = rest[:devices]
    out_ref, fold = rest[devices], rest[devices + 1 :]
    pos = pos_ref[0]
    levels = blocks[0].shape[3] // 4
    half_slots = spec_ref.shape[3]
    jj = perm_ref.shape[0] // 2
    pairs = jj // devices
    tiles = 4 * levels // LANES
    size = pairs * group
    for i, s in enumerate(exchange_order(devices)):
        at = pl.multiple_of((pos ^ s) * size, 8)
        for r in range(2):
            for t in range(tiles):
                block = blocks[i][:, r, :, t * LANES : (t + 1) * LANES].astype(F32)
                fold[r * tiles + t][pl.ds(at, size), :] = block.reshape(size, LANES)
    first = pos * waves + pl.program_id(0) * group
    slot = 2 * lax.broadcasted_iota(jnp.int32, (1, half_slots), 1)
    trunc = trunc_ref[...]
    weight = weight_ref[...]

    def one(m, carry):
        wave = first + m
        turned = []
        for r in range(2):
            at = pl.ds(m, jj, stride=group)
            total = sums_ref[r * waves + pl.program_id(0) * group + m]
            columns = []
            for t in range(tiles):
                share = total * share_ref[:, t * LANES : (t + 1) * LANES]
                columns.append((fold[r * tiles + t][at, :] + share).T)
            turned.append(jnp.concatenate(columns, axis=0))
        rows = []
        for hemi in range(2):
            for r in range(2):
                pieces = []
                for half in range(2):
                    at = (2 * half + hemi) * levels
                    pieces.append(turned[r][at : at + levels])
                rows.append(jnp.concatenate(pieces, axis=1))
        both = jnp.concatenate(rows, axis=0).astype(BF16)
        both = jnp.dot(both, perm_ref[...], preferred_element_type=F32)
        both = jnp.where(trunc > wave, both, 0.0)
        channels = 2 * levels
        north, south = both[:channels], both[channels:]
        for p in range(2):
            folded = (weight * (north + south if p == 0 else north - south)).astype(BF16)
            direct = lax.dot_general(
                folded, basis_ref[m, p], (((1,), (1,)), ((), ())), preferred_element_type=F32
            )
            value = spec_ref[m, p].astype(F32) + direct
            out_ref[m, p] = jnp.where(slot + (wave + p) < 2 * half_slots, value, 0.0).astype(BF16)
        return carry

    lax.fori_loop(0, group, one, 0, unroll=min(group, unroll))


def inverse(pos, sums, spec, basis, trunc, weight, perm, share, blocks, unroll):
    devices = len(blocks)
    waves, _, channels, half_slots = spec.shape
    half_lats = basis.shape[3]
    group = min(8, waves)
    pairs = half_lats // (2 * devices)
    lanes = 2 * channels
    return pl.pallas_call(
        functools.partial(inverse_kernel, devices, group, waves, unroll),
        grid_spec=pltpu.PrefetchScalarGridSpec(
            num_scalar_prefetch=1,
            grid=(waves // group,),
            in_specs=[
                pl.BlockSpec(memory_space=pltpu.SMEM),
                pl.BlockSpec((group, 2, channels, half_slots), lambda i, s: (i, 0, 0, 0)),
                pl.BlockSpec((group, 2, half_slots, half_lats), lambda i, s: (i, 0, 0, 0)),
                pl.BlockSpec((1, half_lats), lambda i, s: (0, 0)),
                pl.BlockSpec((1, half_lats), lambda i, s: (0, 0)),
                pl.BlockSpec((half_lats, half_lats), lambda i, s: (0, 0)),
                pl.BlockSpec((half_lats // 2, lanes), lambda i, s: (0, 0)),
            ]
            + [pl.BlockSpec((pairs, 2, group, lanes), lambda i, s: (0, 0, i, 0))] * devices,
            out_specs=pl.BlockSpec((group, 2, channels, half_slots), lambda i, s: (i, 0, 0, 0)),
            scratch_shapes=[pltpu.VMEM((half_lats // 2 * group, LANES), F32)] * (2 * lanes // LANES),
        ),
        out_shape=jax.ShapeDtypeStruct(spec.shape, BF16),
        compiler_params=params(),
        name="inverse",
    )(pos, sums, spec, basis, trunc, weight, perm, share, *blocks)


def cos_sin(rows, columns):
    phases = rows[:, None] * columns[None, :] % NLON
    angles = phases.astype(F32) * (2.0 * math.pi / NLON)
    return jnp.cos(angles), jnp.sin(angles)


def fourier_tables(waves, lons):
    def outer(rows, columns):
        low = 32
        col = jnp.arange(columns, dtype=jnp.int32)
        small = lax.optimization_barrier(
            cos_sin(jnp.arange(low, dtype=jnp.int32), col)
            + cos_sin(low * jnp.arange(rows // low, dtype=jnp.int32), col)
        )
        c0, s0, c1, s1 = small
        cos = c1[:, None] * c0[None] - s1[:, None] * s0[None]
        sin = s1[:, None] * c0[None] + c1[:, None] * s0[None]
        return cos.reshape(rows, columns).astype(BF16), (-sin).reshape(rows, columns).astype(BF16)

    analysis = jnp.concatenate(outer(waves, lons), axis=0)
    synthesis = jnp.concatenate(outer(lons, waves), axis=1)
    return synthesis, analysis


def exchange(arrays, devices, needed):
    got = [arrays[0]]
    for array, s in list(zip(arrays, exchange_order(devices)))[1:]:
        pairs = [(i, i ^ s) for i in range(devices) if needed(i, i ^ s)]
        got.append(lax.ppermute(array, "wave", pairs))
    return got


def per_device(spectral, basis, quad_weights, column, square_coef, cube_coef, trunc):
    devices = lax.axis_size("wave")
    position = lax.axis_index("wave").astype(jnp.int32)
    waves, _, half_slots, channels = spectral.shape
    half_lats = basis.shape[3]
    levels = channels // 2
    rows = half_lats // devices
    pairs = rows // 2
    pos = position.reshape(1)
    spec = jnp.swapaxes(spectral, 2, 3)
    order = latitude_order(half_lats, devices)
    lats = jnp.arange(half_lats, dtype=jnp.int32)
    perm = (lats[:, None] == order[None, :]).astype(BF16)
    back = (order[:, None] == lats[None, :]).astype(BF16)
    trunc_row = trunc.reshape(1, half_lats)
    weight_row = quad_weights.reshape(1, half_lats)
    blocks = forward(pos, spec, basis, trunc_row, perm, devices)

    reach = [min(devices, g + 1 + max(1, devices // 16)) for g in range(devices)]
    top = jnp.max(trunc.reshape(devices, rows), axis=1)
    fits = jnp.all(top <= waves * jnp.array(reach, dtype=jnp.int32))

    def finish(sparse, blocks):
        def there(source, owner):
            return not sparse or source < reach[devices - 1 - owner]

        def home(owner, source):
            return there(source, owner)

        synthesis, analysis = fourier_tables(devices * waves, NLON)
        sums = jnp.sum(analysis.astype(F32), axis=1, keepdims=True)
        mix = jnp.kron(jnp.eye(4, dtype=F32), column.T).astype(BF16)
        coef = jnp.stack([jnp.tile(square_coef, 4), jnp.tile(cube_coef, 4)])
        group = devices - 1 - position
        own = lax.dynamic_slice(quad_weights, (group * rows,), (rows,)).reshape(2, pairs)
        own = own.T[:, :, None, None]

        got = exchange(blocks, devices, there)
        shifted, means = synthesise(pos, synthesis, mix, coef, got, STEPS if sparse else 1)
        count = pairs // means.shape[0]
        zonal = means[:, 0].reshape(pairs, 2, 2, levels)
        owned = jnp.sum(own * zonal, axis=(0, 1, 2)) / (2.0 * jnp.sum(own))
        excess = means - jnp.tile(owned, 4 * count)
        parts = analyse(
            pos, analysis, sums, shifted, excess, devices, waves, count, STEPS if sparse else 1
        )

        sent = jnp.broadcast_to(jnp.pad(owned, (0, LANES - levels)), (devices, 1, LANES))
        every = lax.all_to_all(sent, "wave", split_axis=0, concat_axis=0, tiled=True)
        every = every[:, 0, :levels]
        held = jnp.sum(quad_weights.reshape(devices, rows)[::-1], axis=1, keepdims=True)
        level_mean = jnp.sum(held * every, axis=0) / jnp.sum(held)
        share = math.sqrt(2.0 / NLON) * jnp.tile(every - level_mean, (1, 4))
        share = jnp.repeat(share, pairs, axis=0)
        kept = lax.dynamic_slice(sums.reshape(2, -1), (0, position * waves), (2, waves))
        parts = exchange(parts, devices, home)
        return inverse(
            pos, kept.reshape(-1), spec, basis, trunc_row, weight_row, back, share, parts,
            8 if sparse else 1,
        )

    out = lax.cond(
        fits, functools.partial(finish, True), functools.partial(finish, False), blocks
    )
    return jnp.swapaxes(out, 2, 3)


def solution(mesh):
    return jax.shard_map(
        per_device,
        mesh=mesh,
        in_specs=(
            P(("member", "wave"), None, None, None),
            P("wave", None, None, None),
            P(),
            P(),
            P(),
            P(),
            P(),
        ),
        out_specs=P(("member", "wave"), None, None, None),
        check_vma=False,
    )
```

```python
import functools
import math

import jax
import jax.numpy as jnp
from jax import lax
from jax.experimental import pallas as pl
from jax.experimental.pallas import tpu as pltpu
from jax.sharding import PartitionSpec as P

NLON = 1024
LANES = 128
F32 = jnp.float32
BF16 = jnp.bfloat16
STEPS = 2
VMEM_LIMIT = 56 * 1024 * 1024


def params():
    return pltpu.CompilerParams(
        dimension_semantics=("arbitrary",), vmem_limit_bytes=VMEM_LIMIT
    )


def latitude_order(half_lats, devices):
    rows = half_lats // devices
    pairs = rows // 2
    lane = jnp.arange(half_lats, dtype=jnp.int32)
    half = lane // (half_lats // 2)
    owner = lane % (half_lats // 2) // pairs
    pair = lane % pairs
    return (devices - 1 - owner) * rows + half * pairs + pair


def exchange_order(devices):
    quarter = max(1, devices // 4)
    order = [0]
    for t in range(quarter):
        order += [2 * quarter + t, quarter + t, 3 * quarter + t]
    return order + list(range(quarter - 1, 0, -1))


def forward_kernel(devices, group, waves, pos_ref, spec_ref, basis_ref, trunc_ref, perm_ref, *rest):
    outs, fold = rest[:devices], rest[devices:]
    pos = pos_ref[0]
    levels = outs[0].shape[3] // 4
    half_slots = spec_ref.shape[3]
    tiles = 4 * levels // LANES
    jj = perm_ref.shape[1] // 2
    pairs = jj // devices
    first = pos * waves + pl.program_id(0) * group
    slot = 2 * lax.broadcasted_iota(jnp.int32, (1, half_slots), 1)
    trunc = trunc_ref[...]

    def one(m, carry):
        wave = first + m
        parity = []
        for p in range(2):
            spec = spec_ref[m, p]
            spec = jnp.where(slot + (wave + p) < 2 * half_slots, spec, jnp.zeros_like(spec))
            parity.append(jnp.dot(spec, basis_ref[m, p], preferred_element_type=F32))
        both = jnp.concatenate([parity[0] + parity[1], parity[0] - parity[1]], axis=0)
        both = jnp.where(trunc > wave, both, 0.0).astype(BF16)
        both = jnp.dot(both, perm_ref[...], preferred_element_type=F32)
        for r in range(2):
            rows = []
            for half in range(2):
                for hemi in range(2):
                    at = (2 * hemi + r) * levels
                    rows.append(both[at : at + levels, half * jj : (half + 1) * jj])
            turned = jnp.concatenate(rows, axis=0).T
            for t in range(tiles):
                at = pl.ds(m, jj, stride=group)
                fold[r * tiles + t][at, :] = turned[:, t * LANES : (t + 1) * LANES]
        return carry

    lax.fori_loop(0, group, one, 0, unroll=group)
    size = pairs * group
    for i, s in enumerate(exchange_order(devices)):
        at = pl.multiple_of((pos ^ s) * size, 8)
        for r in range(2):
            for t in range(tiles):
                block = fold[r * tiles + t][pl.ds(at, size), :].reshape(pairs, group, LANES)
                outs[i][:, r, :, t * LANES : (t + 1) * LANES] = block.astype(BF16)


def forward(pos, spec, basis, trunc, perm, devices):
    waves, _, channels, half_slots = spec.shape
    half_lats = basis.shape[3]
    group = min(8, waves)
    pairs = half_lats // (2 * devices)
    lanes = 2 * channels
    return pl.pallas_call(
        functools.partial(forward_kernel, devices, group, waves),
        grid_spec=pltpu.PrefetchScalarGridSpec(
            num_scalar_prefetch=1,
            grid=(waves // group,),
            in_specs=[
                pl.BlockSpec((group, 2, channels, half_slots), lambda i, s: (i, 0, 0, 0)),
                pl.BlockSpec((group, 2, half_slots, half_lats), lambda i, s: (i, 0, 0, 0)),
                pl.BlockSpec((1, half_lats), lambda i, s: (0, 0)),
                pl.BlockSpec((half_lats, half_lats), lambda i, s: (0, 0)),
            ],
            out_specs=[pl.BlockSpec((pairs, 2, group, lanes), lambda i, s: (0, 0, i, 0))] * devices,
            scratch_shapes=[pltpu.VMEM((half_lats // 2 * group, LANES), F32)] * (2 * lanes // LANES),
        ),
        out_shape=[jax.ShapeDtypeStruct((pairs, 2, waves, lanes), BF16)] * devices,
        compiler_params=params(),
        name="forward",
    )(pos, spec, basis, trunc, perm)


def grid_kernel(devices, waves, unroll, pos_ref, cos_ref, sin_ref, mid_ref, mix_ref, coef_ref, *rest):
    blocks, outs = rest[:devices], rest[devices : 2 * devices]
    mean_ref, coeffs, plus, minus, even, odd = rest[2 * devices :]
    pos = pos_ref[0]
    total = devices * waves
    count, lanes = blocks[0].shape[0], blocks[0].shape[3]
    width = count * lanes
    order = exchange_order(devices)
    for i, s in enumerate(order):
        at = pl.multiple_of((pos ^ s) * waves, 8)
        for r in range(2):
            for c in range(count):
                part = blocks[i][c, r]
                coeffs[pl.ds(r * total + at, waves), c * lanes : (c + 1) * lanes] = part
    half = cos_ref.shape[0]
    step = half // STEPS
    scale = 1.0 / math.sqrt(total)
    middle = jnp.dot(mid_ref[...], coeffs[:total, :], preferred_element_type=F32)[0:1]
    row = lax.broadcasted_iota(jnp.int32, (step, 1), 0)

    def tendency(temp):
        values = []
        for c in range(count):
            mine = temp[:, c * lanes : (c + 1) * lanes]
            mixed = jnp.dot(mine.astype(BF16), mix_ref[...], preferred_element_type=F32)
            values.append(mixed + mine * mine * (coef_ref[0:1, :] - coef_ref[1:2, :] * mine))
        return jnp.concatenate(values, axis=1)

    def one(t, total_sum):
        at = pl.multiple_of(t * step, step)
        cosine = jnp.dot(
            cos_ref[pl.ds(at, step), :], coeffs[:total, :], preferred_element_type=F32
        )
        sine = jnp.dot(
            sin_ref[pl.ds(at, step), :], coeffs[total:, :], preferred_element_type=F32
        )
        first = tendency(scale * (cosine + sine))
        last = tendency(scale * jnp.where(row + at == 0, middle, cosine - sine))
        plus[pl.ds(at, step), :] = first
        minus[pl.ds(at, step), :] = last
        return total_sum + jnp.sum(first + last, axis=0, keepdims=True)

    mean = lax.fori_loop(0, STEPS, one, jnp.zeros((1, width), F32), unroll=unroll)
    mean = mean * (0.5 / half)
    mean_ref[0] = jnp.broadcast_to(mean, mean_ref.shape[1:])
    centre = minus[0:1, :] - mean

    def two(t, carry):
        at = pl.multiple_of(t * step, step)
        first = plus[pl.ds(at, step), :] - mean
        last = jnp.where(row + at == 0, 0.0, minus[pl.ds(at, step), :] - mean)
        even[pl.ds(at, step), :] = (first + last).astype(BF16)
        odd[pl.ds(at, step), :] = (first - last).astype(BF16)
        return carry

    lax.fori_loop(0, STEPS, two, 0, unroll=unroll)
    sign = (1 - 2 * (row % 2)).astype(F32)
    gain = math.sqrt(1.0 / half)

    def three(t, carry):
        at = pl.multiple_of(t * step, step)
        cosine = jnp.dot(cos_ref[pl.ds(at, step), :], even[...], preferred_element_type=F32)
        coeffs[pl.ds(at, step), :] = (gain * (cosine + sign * centre)).astype(BF16)
        sine = jnp.dot(sin_ref[pl.ds(at, step), :], odd[...], preferred_element_type=F32)
        coeffs[pl.ds(total + at, step), :] = (gain * sine).astype(BF16)
        return carry

    lax.fori_loop(0, STEPS, three, 0, unroll=unroll)
    for i, s in enumerate(order):
        at = pl.multiple_of((pos ^ s) * waves, 8)
        for r in range(2):
            for c in range(count):
                part = coeffs[pl.ds(r * total + at, waves), c * lanes : (c + 1) * lanes]
                outs[i][c, r] = part


def on_grid(pos, cosine, sine, middle, mix, coef, blocks, unroll):
    devices = len(blocks)
    pairs, _, waves, lanes = blocks[0].shape
    half, total = cosine.shape
    assert half == total == devices * waves
    count = 2 if pairs % 2 == 0 else 1
    width = count * lanes
    block = pl.BlockSpec((count, 2, waves, lanes), lambda q, s: (q, 0, 0, 0))
    whole = lambda q, s: (0, 0)
    return pl.pallas_call(
        functools.partial(grid_kernel, devices, waves, unroll),
        grid_spec=pltpu.PrefetchScalarGridSpec(
            num_scalar_prefetch=1,
            grid=(pairs // count,),
            in_specs=[
                pl.BlockSpec((half, total), whole),
                pl.BlockSpec((half, total), whole),
                pl.BlockSpec((8, total), whole),
                pl.BlockSpec((lanes, lanes), whole),
                pl.BlockSpec((2, lanes), whole),
            ]
            + [block] * devices,
            out_specs=[block] * devices + [pl.BlockSpec((1, 8, width), lambda q, s: (q, 0, 0))],
            scratch_shapes=[
                pltpu.VMEM((2 * total, width), BF16),
                pltpu.VMEM((half, width), F32),
                pltpu.VMEM((half, width), F32),
                pltpu.VMEM((half, width), BF16),
                pltpu.VMEM((half, width), BF16),
            ],
        ),
        out_shape=[jax.ShapeDtypeStruct(blocks[0].shape, BF16)] * devices
        + [jax.ShapeDtypeStruct((pairs // count, 8, width), F32)],
        compiler_params=params(),
        name="grid",
    )(pos, cosine, sine, middle, mix, coef, *blocks)


def inverse_kernel(
    devices, group, waves, unroll, pos_ref, sums_ref, spec_ref, basis_ref, trunc_ref, weight_ref, perm_ref,
    share_ref, *rest
):
    blocks = rest[:devices]
    out_ref, fold = rest[devices], rest[devices + 1 :]
    pos = pos_ref[0]
    levels = blocks[0].shape[3] // 4
    half_slots = spec_ref.shape[3]
    jj = perm_ref.shape[0] // 2
    pairs = jj // devices
    tiles = 4 * levels // LANES
    size = pairs * group
    for i, s in enumerate(exchange_order(devices)):
        at = pl.multiple_of((pos ^ s) * size, 8)
        for r in range(2):
            for t in range(tiles):
                block = blocks[i][:, r, :, t * LANES : (t + 1) * LANES].astype(F32)
                fold[r * tiles + t][pl.ds(at, size), :] = block.reshape(size, LANES)
    first = pos * waves + pl.program_id(0) * group
    slot = 2 * lax.broadcasted_iota(jnp.int32, (1, half_slots), 1)
    trunc = trunc_ref[...]
    weight = weight_ref[...]

    def one(m, carry):
        wave = first + m
        turned = []
        for r in range(2):
            at = pl.ds(m, jj, stride=group)
            total = sums_ref[r * waves + pl.program_id(0) * group + m]
            columns = []
            for t in range(tiles):
                share = total * share_ref[:, t * LANES : (t + 1) * LANES]
                columns.append((fold[r * tiles + t][at, :] + share).T)
            turned.append(jnp.concatenate(columns, axis=0))
        rows = []
        for hemi in range(2):
            for r in range(2):
                pieces = []
                for half in range(2):
                    at = (2 * half + hemi) * levels
                    pieces.append(turned[r][at : at + levels])
                rows.append(jnp.concatenate(pieces, axis=1))
        both = jnp.concatenate(rows, axis=0).astype(BF16)
        both = jnp.dot(both, perm_ref[...], preferred_element_type=F32)
        both = jnp.where(trunc > wave, both, 0.0)
        channels = 2 * levels
        north, south = both[:channels], both[channels:]
        for p in range(2):
            folded = (weight * (north + south if p == 0 else north - south)).astype(BF16)
            direct = lax.dot_general(
                folded, basis_ref[m, p], (((1,), (1,)), ((), ())), preferred_element_type=F32
            )
            value = spec_ref[m, p].astype(F32) + direct
            out_ref[m, p] = jnp.where(slot + (wave + p) < 2 * half_slots, value, 0.0).astype(BF16)
        return carry

    lax.fori_loop(0, group, one, 0, unroll=min(group, unroll))


def inverse(pos, sums, spec, basis, trunc, weight, perm, share, blocks, unroll):
    devices = len(blocks)
    waves, _, channels, half_slots = spec.shape
    half_lats = basis.shape[3]
    group = min(8, waves)
    pairs = half_lats // (2 * devices)
    lanes = 2 * channels
    return pl.pallas_call(
        functools.partial(inverse_kernel, devices, group, waves, unroll),
        grid_spec=pltpu.PrefetchScalarGridSpec(
            num_scalar_prefetch=1,
            grid=(waves // group,),
            in_specs=[
                pl.BlockSpec(memory_space=pltpu.SMEM),
                pl.BlockSpec((group, 2, channels, half_slots), lambda i, s: (i, 0, 0, 0)),
                pl.BlockSpec((group, 2, half_slots, half_lats), lambda i, s: (i, 0, 0, 0)),
                pl.BlockSpec((1, half_lats), lambda i, s: (0, 0)),
                pl.BlockSpec((1, half_lats), lambda i, s: (0, 0)),
                pl.BlockSpec((half_lats, half_lats), lambda i, s: (0, 0)),
                pl.BlockSpec((half_lats // 2, lanes), lambda i, s: (0, 0)),
            ]
            + [pl.BlockSpec((pairs, 2, group, lanes), lambda i, s: (0, 0, i, 0))] * devices,
            out_specs=pl.BlockSpec((group, 2, channels, half_slots), lambda i, s: (i, 0, 0, 0)),
            scratch_shapes=[pltpu.VMEM((half_lats // 2 * group, LANES), F32)] * (2 * lanes // LANES),
        ),
        out_shape=jax.ShapeDtypeStruct(spec.shape, BF16),
        compiler_params=params(),
        name="inverse",
    )(pos, sums, spec, basis, trunc, weight, perm, share, *blocks)


def cos_sin(rows, columns):
    phases = rows[:, None] * columns[None, :] % NLON
    angles = phases.astype(F32) * (2.0 * math.pi / NLON)
    return jnp.cos(angles), jnp.sin(angles)


def fourier_tables(size):
    low = 32
    col = jnp.arange(size, dtype=jnp.int32)
    c0, s0, c1, s1 = lax.optimization_barrier(
        cos_sin(jnp.arange(low, dtype=jnp.int32), col)
        + cos_sin(low * jnp.arange(size // low, dtype=jnp.int32), col)
    )
    cos = c1[:, None] * c0[None] - s1[:, None] * s0[None]
    sin = s1[:, None] * c0[None] + c1[:, None] * s0[None]
    return cos.reshape(size, size).astype(BF16), (-sin).reshape(size, size).astype(BF16)


def exchange(arrays, devices, needed):
    got = [arrays[0]]
    for array, s in list(zip(arrays, exchange_order(devices)))[1:]:
        pairs = [(i, i ^ s) for i in range(devices) if needed(i, i ^ s)]
        got.append(lax.ppermute(array, "wave", pairs))
    return got


def per_device(spectral, basis, quad_weights, column, square_coef, cube_coef, trunc):
    devices = lax.axis_size("wave")
    position = lax.axis_index("wave").astype(jnp.int32)
    waves, _, half_slots, channels = spectral.shape
    half_lats = basis.shape[3]
    levels = channels // 2
    rows = half_lats // devices
    pairs = rows // 2
    pos = position.reshape(1)
    spec = jnp.swapaxes(spectral, 2, 3)
    order = latitude_order(half_lats, devices)
    lats = jnp.arange(half_lats, dtype=jnp.int32)
    perm = (lats[:, None] == order[None, :]).astype(BF16)
    back = (order[:, None] == lats[None, :]).astype(BF16)
    trunc_row = trunc.reshape(1, half_lats)
    weight_row = quad_weights.reshape(1, half_lats)
    blocks = forward(pos, spec, basis, trunc_row, perm, devices)

    reach = [min(devices, g + 1 + max(1, devices // 16)) for g in range(devices)]
    top = jnp.max(trunc.reshape(devices, rows), axis=1)
    fits = jnp.all(top <= waves * jnp.array(reach, dtype=jnp.int32))

    def finish(sparse, blocks):
        def there(source, owner):
            return not sparse or source < reach[devices - 1 - owner]

        def home(owner, source):
            return there(source, owner)

        total = devices * waves
        cosine, sine = fourier_tables(total)
        sign = 1 - 2 * (jnp.arange(total, dtype=jnp.int32) % 2)
        middle = jnp.broadcast_to(sign.astype(BF16), (8, total))
        mix = jnp.kron(jnp.eye(4, dtype=F32), column.T).astype(BF16)
        coef = jnp.stack([jnp.tile(square_coef, 4), jnp.tile(cube_coef, 4)])
        sums = 2.0 * jnp.sum(cosine.astype(F32), axis=1) - cosine[:, 0].astype(F32)
        sums = jnp.stack([sums + sign.astype(F32), jnp.zeros((total,), F32)])
        kept = lax.dynamic_slice(sums, (0, position * waves), (2, waves)).reshape(-1)
        held = jnp.swapaxes(quad_weights.reshape(devices, 2, pairs)[::-1], 1, 2)
        held = held.reshape(devices * pairs, 2, 1, 1) / (2.0 * jnp.sum(quad_weights))

        got = exchange(blocks, devices, there)
        *parts, means = on_grid(
            pos, cosine, sine, middle, mix, coef, got, STEPS if sparse else 1
        )
        parts = exchange(parts, devices, home)

        sent = means[:, 0].reshape(1, -1, LANES)
        sent = jnp.broadcast_to(sent, (devices,) + sent.shape[1:])
        sent, parts[-1] = lax.optimization_barrier((sent, parts[-1]))
        every = lax.all_to_all(sent, "wave", split_axis=0, concat_axis=0, tiled=True)
        every = every.reshape(devices * pairs, 4 * levels)
        level_mean = jnp.sum(held * every.reshape(-1, 2, 2, levels), axis=(0, 1, 2))
        share = math.sqrt(2.0 / NLON) * (every - jnp.tile(level_mean, 4))
        return inverse(
            pos, kept, spec, basis, trunc_row, weight_row, back, share, parts,
            8 if sparse else 1,
        )

    out = lax.cond(
        fits, functools.partial(finish, True), functools.partial(finish, False), blocks
    )
    return jnp.swapaxes(out, 2, 3)


def solution(mesh):
    return jax.shard_map(
        per_device,
        mesh=mesh,
        in_specs=(
            P(("member", "wave"), None, None, None),
            P("wave", None, None, None),
            P(),
            P(),
            P(),
            P(),
            P(),
        ),
        out_specs=P(("member", "wave"), None, None, None),
        check_vma=False,
    )
```

```python
import functools
import math

import jax
import jax.numpy as jnp
from jax import lax
from jax.experimental import pallas as pl
from jax.experimental.pallas import tpu as pltpu
from jax.sharding import PartitionSpec as P


NLON = 1024
LANES = 128
F32 = jnp.float32
BF16 = jnp.bfloat16
STEPS = 2
VMEM_LIMIT = 56 * 1024 * 1024


def params():
    return pltpu.CompilerParams(
        dimension_semantics=("arbitrary",), vmem_limit_bytes=VMEM_LIMIT
    )


def owned_groups(devices):
    turn = (0, 3, 1, 2) if devices % 4 == 0 else tuple(range(devices))
    size = len(turn)
    return [devices - 1 - (e // size * size + turn[e % size]) for e in range(devices)]


def latitude_order(half_lats, devices):
    rows = half_lats // devices
    pairs = rows // 2
    lane = jnp.arange(half_lats, dtype=jnp.int32)
    half = lane // (half_lats // 2)
    owner = lane % (half_lats // 2) // pairs
    pair = lane % pairs
    groups = jnp.array(owned_groups(devices), dtype=jnp.int32)
    group = jnp.sum(jnp.where(owner[:, None] == jnp.arange(devices), groups[None, :], 0), axis=1)
    return group * rows + half * pairs + pair


def exchange_order(devices):
    quarter = max(1, devices // 4)
    order = [0]
    for t in range(quarter):
        order += [2 * quarter + t, quarter + t, 3 * quarter + t]
    return order + list(range(quarter - 1, 0, -1))


def forward_kernel(devices, group, waves, pos_ref, spec_ref, basis_ref, trunc_ref, perm_ref, *rest):
    outs, fold = rest[:devices], rest[devices:]
    pos = pos_ref[0]
    levels = outs[0].shape[3] // 4
    half_slots = spec_ref.shape[3]
    tiles = 4 * levels // LANES
    jj = perm_ref.shape[1] // 2
    pairs = jj // devices
    first = pos * waves + pl.program_id(0) * group
    slot = 2 * lax.broadcasted_iota(jnp.int32, (1, half_slots), 1)
    trunc = trunc_ref[...]

    def one(m, carry):
        wave = first + m
        parity = []
        for p in range(2):
            spec = spec_ref[m, p]
            spec = jnp.where(slot + (wave + p) < 2 * half_slots, spec, jnp.zeros_like(spec))
            parity.append(jnp.dot(spec, basis_ref[m, p], preferred_element_type=F32))
        both = jnp.concatenate([parity[0] + parity[1], parity[0] - parity[1]], axis=0)
        both = jnp.where(trunc > wave, both, 0.0).astype(BF16)
        both = jnp.dot(both, perm_ref[...], preferred_element_type=F32)
        for r in range(2):
            rows = []
            for half in range(2):
                for hemi in range(2):
                    at = (2 * hemi + r) * levels
                    rows.append(both[at : at + levels, half * jj : (half + 1) * jj])
            turned = jnp.concatenate(rows, axis=0).T
            for t in range(tiles):
                at = pl.ds(m, jj, stride=group)
                fold[r * tiles + t][at, :] = turned[:, t * LANES : (t + 1) * LANES]
        return carry

    lax.fori_loop(0, group, one, 0, unroll=group)
    size = pairs * group
    for i, s in enumerate(exchange_order(devices)):
        at = pl.multiple_of((pos ^ s) * size, 8)
        for r in range(2):
            for t in range(tiles):
                block = fold[r * tiles + t][pl.ds(at, size), :].reshape(pairs, group, LANES)
                outs[i][:, r, :, t * LANES : (t + 1) * LANES] = block.astype(BF16)


def forward(pos, spec, basis, trunc, perm, devices):
    waves, _, channels, half_slots = spec.shape
    half_lats = basis.shape[3]
    group = min(8, waves)
    pairs = half_lats // (2 * devices)
    lanes = 2 * channels
    return pl.pallas_call(
        functools.partial(forward_kernel, devices, group, waves),
        grid_spec=pltpu.PrefetchScalarGridSpec(
            num_scalar_prefetch=1,
            grid=(waves // group,),
            in_specs=[
                pl.BlockSpec((group, 2, channels, half_slots), lambda i, s: (i, 0, 0, 0)),
                pl.BlockSpec((group, 2, half_slots, half_lats), lambda i, s: (i, 0, 0, 0)),
                pl.BlockSpec((1, half_lats), lambda i, s: (0, 0)),
                pl.BlockSpec((half_lats, half_lats), lambda i, s: (0, 0)),
            ],
            out_specs=[pl.BlockSpec((pairs, 2, group, lanes), lambda i, s: (0, 0, i, 0))] * devices,
            scratch_shapes=[pltpu.VMEM((half_lats // 2 * group, LANES), F32)] * (2 * lanes // LANES),
        ),
        out_shape=[jax.ShapeDtypeStruct((pairs, 2, waves, lanes), BF16)] * devices,
        compiler_params=params(),
        name="forward",
    )(pos, spec, basis, trunc, perm)


def grid_kernel(devices, waves, unroll, pos_ref, cos_ref, sin_ref, mid_ref, mix_ref, coef_ref, *rest):
    blocks, outs = rest[:devices], rest[devices : 2 * devices]
    mean_ref, coeffs, plus, minus, even, odd = rest[2 * devices :]
    pos = pos_ref[0]
    total = devices * waves
    count, lanes = blocks[0].shape[0], blocks[0].shape[3]
    width = count * lanes
    order = exchange_order(devices)
    for i, s in enumerate(order):
        at = pl.multiple_of((pos ^ s) * waves, 8)
        for r in range(2):
            for c in range(count):
                part = blocks[i][c, r]
                coeffs[pl.ds(r * total + at, waves), c * lanes : (c + 1) * lanes] = part
    half = cos_ref.shape[0]
    step = half // STEPS
    scale = 1.0 / math.sqrt(total)
    middle = jnp.dot(mid_ref[...], coeffs[:total, :], preferred_element_type=F32)[0:1]
    row = lax.broadcasted_iota(jnp.int32, (step, 1), 0)

    def tendency(temp):
        values = []
        for c in range(count):
            mine = temp[:, c * lanes : (c + 1) * lanes]
            mixed = jnp.dot(mine.astype(BF16), mix_ref[...], preferred_element_type=F32)
            values.append(mixed + mine * mine * (coef_ref[0:1, :] - coef_ref[1:2, :] * mine))
        return jnp.concatenate(values, axis=1)

    def one(t, total_sum):
        at = pl.multiple_of(t * step, step)
        cosine = jnp.dot(
            cos_ref[pl.ds(at, step), :], coeffs[:total, :], preferred_element_type=F32
        )
        sine = jnp.dot(
            sin_ref[pl.ds(at, step), :], coeffs[total:, :], preferred_element_type=F32
        )
        first = tendency(scale * (cosine + sine))
        last = tendency(scale * jnp.where(row + at == 0, middle, cosine - sine))
        plus[pl.ds(at, step), :] = first
        minus[pl.ds(at, step), :] = last
        return total_sum + jnp.sum(first + last, axis=0, keepdims=True)

    mean = lax.fori_loop(0, STEPS, one, jnp.zeros((1, width), F32), unroll=unroll)
    mean = mean * (0.5 / half)
    mean_ref[0] = jnp.broadcast_to(mean, mean_ref.shape[1:])
    centre = minus[0:1, :] - mean

    def two(t, carry):
        at = pl.multiple_of(t * step, step)
        first = plus[pl.ds(at, step), :] - mean
        last = jnp.where(row + at == 0, 0.0, minus[pl.ds(at, step), :] - mean)
        even[pl.ds(at, step), :] = (first + last).astype(BF16)
        odd[pl.ds(at, step), :] = (first - last).astype(BF16)
        return carry

    lax.fori_loop(0, STEPS, two, 0, unroll=unroll)
    sign = (1 - 2 * (row % 2)).astype(F32)
    gain = math.sqrt(1.0 / half)

    def three(t, carry):
        at = pl.multiple_of(t * step, step)
        cosine = jnp.dot(cos_ref[pl.ds(at, step), :], even[...], preferred_element_type=F32)
        coeffs[pl.ds(at, step), :] = (gain * (cosine + sign * centre)).astype(BF16)
        sine = jnp.dot(sin_ref[pl.ds(at, step), :], odd[...], preferred_element_type=F32)
        coeffs[pl.ds(total + at, step), :] = (gain * sine).astype(BF16)
        return carry

    lax.fori_loop(0, STEPS, three, 0, unroll=unroll)
    for i, s in enumerate(order):
        at = pl.multiple_of((pos ^ s) * waves, 8)
        for r in range(2):
            for c in range(count):
                part = coeffs[pl.ds(r * total + at, waves), c * lanes : (c + 1) * lanes]
                outs[i][c, r] = part


def on_grid(pos, cosine, sine, middle, mix, coef, blocks, unroll):
    devices = len(blocks)
    pairs, _, waves, lanes = blocks[0].shape
    half, total = cosine.shape
    assert half == total == devices * waves
    count = 2 if pairs % 2 == 0 else 1
    width = count * lanes
    block = pl.BlockSpec((count, 2, waves, lanes), lambda q, s: (q, 0, 0, 0))
    whole = lambda q, s: (0, 0)
    return pl.pallas_call(
        functools.partial(grid_kernel, devices, waves, unroll),
        grid_spec=pltpu.PrefetchScalarGridSpec(
            num_scalar_prefetch=1,
            grid=(pairs // count,),
            in_specs=[
                pl.BlockSpec((half, total), whole),
                pl.BlockSpec((half, total), whole),
                pl.BlockSpec((8, total), whole),
                pl.BlockSpec((lanes, lanes), whole),
                pl.BlockSpec((2, lanes), whole),
            ]
            + [block] * devices,
            out_specs=[block] * devices + [pl.BlockSpec((1, 8, width), lambda q, s: (q, 0, 0))],
            scratch_shapes=[
                pltpu.VMEM((2 * total, width), BF16),
                pltpu.VMEM((half, width), F32),
                pltpu.VMEM((half, width), F32),
                pltpu.VMEM((half, width), BF16),
                pltpu.VMEM((half, width), BF16),
            ],
        ),
        out_shape=[jax.ShapeDtypeStruct(blocks[0].shape, BF16)] * devices
        + [jax.ShapeDtypeStruct((pairs // count, 8, width), F32)],
        compiler_params=params(),
        name="grid",
    )(pos, cosine, sine, middle, mix, coef, *blocks)


def inverse_kernel(
    devices, group, waves, unroll, pos_ref, sums_ref, spec_ref, basis_ref, trunc_ref, weight_ref, perm_ref,
    share_ref, *rest
):
    blocks = rest[:devices]
    out_ref, fold = rest[devices], rest[devices + 1 :]
    pos = pos_ref[0]
    levels = blocks[0].shape[3] // 4
    half_slots = spec_ref.shape[3]
    jj = perm_ref.shape[0] // 2
    pairs = jj // devices
    tiles = 4 * levels // LANES
    size = pairs * group
    for i, s in enumerate(exchange_order(devices)):
        at = pl.multiple_of((pos ^ s) * size, 8)
        for r in range(2):
            for t in range(tiles):
                block = blocks[i][:, r, :, t * LANES : (t + 1) * LANES].astype(F32)
                fold[r * tiles + t][pl.ds(at, size), :] = block.reshape(size, LANES)
    first = pos * waves + pl.program_id(0) * group
    slot = 2 * lax.broadcasted_iota(jnp.int32, (1, half_slots), 1)
    trunc = trunc_ref[...]
    weight = weight_ref[...]

    def one(m, carry):
        wave = first + m
        turned = []
        for r in range(2):
            at = pl.ds(m, jj, stride=group)
            total = sums_ref[r * waves + pl.program_id(0) * group + m]
            columns = []
            for t in range(tiles):
                share = total * share_ref[:, t * LANES : (t + 1) * LANES]
                columns.append((fold[r * tiles + t][at, :] + share).T)
            turned.append(jnp.concatenate(columns, axis=0))
        rows = []
        for hemi in range(2):
            for r in range(2):
                pieces = []
                for half in range(2):
                    at = (2 * half + hemi) * levels
                    pieces.append(turned[r][at : at + levels])
                rows.append(jnp.concatenate(pieces, axis=1))
        both = jnp.concatenate(rows, axis=0).astype(BF16)
        both = jnp.dot(both, perm_ref[...], preferred_element_type=F32)
        both = jnp.where(trunc > wave, both, 0.0)
        channels = 2 * levels
        north, south = both[:channels], both[channels:]
        for p in range(2):
            folded = (weight * (north + south if p == 0 else north - south)).astype(BF16)
            direct = lax.dot_general(
                folded, basis_ref[m, p], (((1,), (1,)), ((), ())), preferred_element_type=F32
            )
            value = spec_ref[m, p].astype(F32) + direct
            out_ref[m, p] = jnp.where(slot + (wave + p) < 2 * half_slots, value, 0.0).astype(BF16)
        return carry

    lax.fori_loop(0, group, one, 0, unroll=min(group, unroll))


def inverse(pos, sums, spec, basis, trunc, weight, perm, share, blocks, unroll):
    devices = len(blocks)
    waves, _, channels, half_slots = spec.shape
    half_lats = basis.shape[3]
    group = min(8, waves)
    pairs = half_lats // (2 * devices)
    lanes = 2 * channels
    return pl.pallas_call(
        functools.partial(inverse_kernel, devices, group, waves, unroll),
        grid_spec=pltpu.PrefetchScalarGridSpec(
            num_scalar_prefetch=1,
            grid=(waves // group,),
            in_specs=[
                pl.BlockSpec(memory_space=pltpu.SMEM),
                pl.BlockSpec((group, 2, channels, half_slots), lambda i, s: (i, 0, 0, 0)),
                pl.BlockSpec((group, 2, half_slots, half_lats), lambda i, s: (i, 0, 0, 0)),
                pl.BlockSpec((1, half_lats), lambda i, s: (0, 0)),
                pl.BlockSpec((1, half_lats), lambda i, s: (0, 0)),
                pl.BlockSpec((half_lats, half_lats), lambda i, s: (0, 0)),
                pl.BlockSpec((half_lats // 2, lanes), lambda i, s: (0, 0)),
            ]
            + [pl.BlockSpec((pairs, 2, group, lanes), lambda i, s: (0, 0, i, 0))] * devices,
            out_specs=pl.BlockSpec((group, 2, channels, half_slots), lambda i, s: (i, 0, 0, 0)),
            scratch_shapes=[pltpu.VMEM((half_lats // 2 * group, LANES), F32)] * (2 * lanes // LANES),
        ),
        out_shape=jax.ShapeDtypeStruct(spec.shape, BF16),
        compiler_params=params(),
        name="inverse",
    )(pos, sums, spec, basis, trunc, weight, perm, share, *blocks)


def cos_sin(rows, columns):
    phases = rows[:, None] * columns[None, :] % NLON
    angles = phases.astype(F32) * (2.0 * math.pi / NLON)
    return jnp.cos(angles), jnp.sin(angles)


def fourier_tables(size):
    low = 32
    col = jnp.arange(size, dtype=jnp.int32)
    c0, s0, c1, s1 = lax.optimization_barrier(
        cos_sin(jnp.arange(low, dtype=jnp.int32), col)
        + cos_sin(low * jnp.arange(size // low, dtype=jnp.int32), col)
    )
    cos = c1[:, None] * c0[None] - s1[:, None] * s0[None]
    sin = s1[:, None] * c0[None] + c1[:, None] * s0[None]
    return cos.reshape(size, size).astype(BF16), (-sin).reshape(size, size).astype(BF16)


def exchange(arrays, devices, needed):
    got = [arrays[0]]
    for array, s in list(zip(arrays, exchange_order(devices)))[1:]:
        pairs = [(i, i ^ s) for i in range(devices) if needed(i, i ^ s)]
        got.append(lax.ppermute(array, "wave", pairs))
    return got


def per_device(spectral, basis, quad_weights, column, square_coef, cube_coef, trunc):
    devices = lax.axis_size("wave")
    position = lax.axis_index("wave").astype(jnp.int32)
    waves, _, _, channels = spectral.shape
    half_lats = basis.shape[3]
    levels = channels // 2
    rows = half_lats // devices
    pairs = rows // 2
    pos = position.reshape(1)
    spec = jnp.swapaxes(spectral, 2, 3)
    order = latitude_order(half_lats, devices)
    lats = jnp.arange(half_lats, dtype=jnp.int32)
    perm = (lats[:, None] == order[None, :]).astype(BF16)
    back = (order[:, None] == lats[None, :]).astype(BF16)
    trunc_row = trunc.reshape(1, half_lats)
    weight_row = quad_weights.reshape(1, half_lats)
    blocks = forward(pos, spec, basis, trunc_row, perm, devices)

    groups = owned_groups(devices)
    reach = [min(devices, g + 1 + max(1, devices // 16)) for g in range(devices)]
    top = jnp.max(trunc.reshape(devices, rows), axis=1)
    fits = jnp.all(top <= waves * jnp.array(reach, dtype=jnp.int32))

    def finish(sparse, blocks):
        def there(source, owner):
            return not sparse or source < reach[groups[owner]]

        def home(owner, source):
            return there(source, owner)

        total = devices * waves
        cosine, sine = fourier_tables(total)
        sign = 1 - 2 * (jnp.arange(total, dtype=jnp.int32) % 2)
        middle = jnp.broadcast_to(sign.astype(BF16), (8, total))
        mix = jnp.kron(jnp.eye(4, dtype=F32), column.T).astype(BF16)
        coef = jnp.stack([jnp.tile(square_coef, 4), jnp.tile(cube_coef, 4)])
        sums = 2.0 * jnp.sum(cosine.astype(F32), axis=1) - cosine[:, 0].astype(F32)
        sums = jnp.stack([sums + sign.astype(F32), jnp.zeros((total,), F32)])
        kept = lax.dynamic_slice(sums, (0, position * waves), (2, waves)).reshape(-1)
        held = quad_weights.reshape(devices, 2, pairs)
        held = jnp.swapaxes(jnp.stack([held[g] for g in groups]), 1, 2)
        held = held.reshape(devices * pairs, 2, 1, 1) / (2.0 * jnp.sum(quad_weights))

        got = exchange(blocks, devices, there)
        *parts, means = on_grid(
            pos, cosine, sine, middle, mix, coef, got, STEPS if sparse else 1
        )
        parts = exchange(parts, devices, home)

        sent = means[:, 0].reshape(1, -1, LANES)
        sent = jnp.broadcast_to(sent, (devices,) + sent.shape[1:])
        every = lax.all_to_all(sent, "wave", split_axis=0, concat_axis=0, tiled=True)
        every = every.reshape(devices * pairs, 4 * levels)
        level_mean = jnp.sum(held * every.reshape(-1, 2, 2, levels), axis=(0, 1, 2))
        share = math.sqrt(2.0 / NLON) * (every - jnp.tile(level_mean, 4))
        return inverse(
            pos, kept, spec, basis, trunc_row, weight_row, back, share, parts,
            8 if sparse else 1,
        )

    def sparse(blocks):
        return finish(True, blocks)

    def dense(blocks):
        return finish(False, blocks)

    out = lax.cond(fits, sparse, dense, blocks)
    return jnp.swapaxes(out, 2, 3)


def solution(mesh):
    return jax.shard_map(
        per_device,
        mesh=mesh,
        in_specs=(
            P(("member", "wave"), None, None, None),
            P("wave", None, None, None),
            P(),
            P(),
            P(),
            P(),
            P(),
        ),
        out_specs=P(("member", "wave"), None, None, None),
        check_vma=False,
    )
```

```python
import functools
import math

import jax
import jax.numpy as jnp
import numpy as np
from jax import lax
from jax.experimental import pallas as pl
from jax.experimental.pallas import tpu as pltpu
from jax.sharding import PartitionSpec as P


NLON = 1024
LANES = 128
F32 = jnp.float32
BF16 = jnp.bfloat16
STEPS = 2
VMEM_LIMIT = 56 * 1024 * 1024


def params():
    return pltpu.CompilerParams(
        dimension_semantics=("arbitrary",), vmem_limit_bytes=VMEM_LIMIT
    )


def owned_groups(devices):
    turn = (0, 3, 1, 2) if devices % 4 == 0 else tuple(range(devices))
    size = len(turn)
    return [devices - 1 - (e // size * size + turn[e % size]) for e in range(devices)]


def latitude_order(half_lats, devices):
    rows = half_lats // devices
    pairs = rows // 2
    lane = np.arange(half_lats)
    half = lane // (half_lats // 2)
    owner = lane % (half_lats // 2) // pairs
    group = np.array(owned_groups(devices))[owner]
    return (group * rows + half * pairs + lane % pairs).astype(np.int32)


def exchange_order(devices):
    quarter = max(1, devices // 4)
    order = [0]
    for t in range(quarter):
        order += [2 * quarter + t, quarter + t, 3 * quarter + t]
    return order + list(range(quarter - 1, 0, -1))


def forward_kernel(devices, group, waves, pos_ref, spec_ref, basis_ref, trunc_ref, perm_ref, *rest):
    outs, fold = rest[:devices], rest[devices:]
    pos = pos_ref[0]
    levels = outs[0].shape[3] // 4
    half_slots = spec_ref.shape[3]
    tiles = 4 * levels // LANES
    jj = perm_ref.shape[1] // 2
    pairs = jj // devices
    first = pos * waves + pl.program_id(0) * group
    slot = 2 * lax.broadcasted_iota(jnp.int32, (1, half_slots), 1)
    trunc = trunc_ref[...]

    def one(m, carry):
        wave = first + m
        parity = []
        for p in range(2):
            spec = spec_ref[m, p]
            spec = jnp.where(slot + (wave + p) < 2 * half_slots, spec, jnp.zeros_like(spec))
            parity.append(jnp.dot(spec, basis_ref[m, p], preferred_element_type=F32))
        both = jnp.concatenate([parity[0] + parity[1], parity[0] - parity[1]], axis=0)
        both = jnp.where(trunc > wave, both, 0.0).astype(BF16)
        both = jnp.dot(both, perm_ref[...], preferred_element_type=F32)
        for r in range(2):
            rows = []
            for half in range(2):
                for hemi in range(2):
                    at = (2 * hemi + r) * levels
                    rows.append(both[at : at + levels, half * jj : (half + 1) * jj])
            turned = jnp.concatenate(rows, axis=0).T
            for t in range(tiles):
                at = pl.ds(m, jj, stride=group)
                fold[r * tiles + t][at, :] = turned[:, t * LANES : (t + 1) * LANES]
        return carry

    lax.fori_loop(0, group, one, 0, unroll=group)
    size = pairs * group
    for i, s in enumerate(exchange_order(devices)):
        at = pl.multiple_of((pos ^ s) * size, 8)
        for r in range(2):
            for t in range(tiles):
                block = fold[r * tiles + t][pl.ds(at, size), :].reshape(pairs, group, LANES)
                outs[i][:, r, :, t * LANES : (t + 1) * LANES] = block.astype(BF16)


def forward(pos, spec, basis, trunc, perm, devices):
    waves, _, channels, half_slots = spec.shape
    half_lats = basis.shape[3]
    group = min(8, waves)
    pairs = half_lats // (2 * devices)
    lanes = 2 * channels
    return pl.pallas_call(
        functools.partial(forward_kernel, devices, group, waves),
        grid_spec=pltpu.PrefetchScalarGridSpec(
            num_scalar_prefetch=1,
            grid=(waves // group,),
            in_specs=[
                pl.BlockSpec((group, 2, channels, half_slots), lambda i, s: (i, 0, 0, 0)),
                pl.BlockSpec((group, 2, half_slots, half_lats), lambda i, s: (i, 0, 0, 0)),
                pl.BlockSpec((1, half_lats), lambda i, s: (0, 0)),
                pl.BlockSpec((half_lats, half_lats), lambda i, s: (0, 0)),
            ],
            out_specs=[pl.BlockSpec((pairs, 2, group, lanes), lambda i, s: (0, 0, i, 0))] * devices,
            scratch_shapes=[pltpu.VMEM((half_lats // 2 * group, LANES), F32)] * (2 * lanes // LANES),
        ),
        out_shape=[jax.ShapeDtypeStruct((pairs, 2, waves, lanes), BF16)] * devices,
        compiler_params=params(),
        name="forward",
    )(pos, spec, basis, trunc, perm)


def grid_kernel(devices, waves, unroll, pos_ref, cos_ref, sin_ref, mid_ref, mix_ref, coef_ref, *rest):
    blocks, outs = rest[:devices], rest[devices : 2 * devices]
    mean_ref, coeffs, plus, minus, even, odd = rest[2 * devices :]
    pos = pos_ref[0]
    total = devices * waves
    count, lanes = blocks[0].shape[0], blocks[0].shape[3]
    width = count * lanes
    order = exchange_order(devices)
    for i, s in enumerate(order):
        at = pl.multiple_of((pos ^ s) * waves, 8)
        for r in range(2):
            for c in range(count):
                part = blocks[i][c, r]
                coeffs[pl.ds(r * total + at, waves), c * lanes : (c + 1) * lanes] = part
    half = cos_ref.shape[0]
    step = half // STEPS
    scale = 1.0 / math.sqrt(total)
    middle = jnp.dot(mid_ref[...], coeffs[:total, :], preferred_element_type=F32)[0:1]
    row = lax.broadcasted_iota(jnp.int32, (step, 1), 0)

    def tendency(temp):
        values = []
        for c in range(count):
            mine = temp[:, c * lanes : (c + 1) * lanes]
            mixed = jnp.dot(mine.astype(BF16), mix_ref[...], preferred_element_type=F32)
            values.append(mixed + mine * mine * (coef_ref[0:1, :] - coef_ref[1:2, :] * mine))
        return jnp.concatenate(values, axis=1)

    def one(t, total_sum):
        at = pl.multiple_of(t * step, step)
        cosine = jnp.dot(
            cos_ref[pl.ds(at, step), :], coeffs[:total, :], preferred_element_type=F32
        )
        sine = jnp.dot(
            sin_ref[pl.ds(at, step), :], coeffs[total:, :], preferred_element_type=F32
        )
        first = tendency(scale * (cosine + sine))
        last = tendency(scale * jnp.where(row + at == 0, middle, cosine - sine))
        plus[pl.ds(at, step), :] = first
        minus[pl.ds(at, step), :] = last
        return total_sum + jnp.sum(first + last, axis=0, keepdims=True)

    mean = lax.fori_loop(0, STEPS, one, jnp.zeros((1, width), F32), unroll=unroll)
    mean = mean * (0.5 / half)
    mean_ref[0] = jnp.broadcast_to(mean, mean_ref.shape[1:])
    centre = minus[0:1, :] - mean

    def two(t, carry):
        at = pl.multiple_of(t * step, step)
        first = plus[pl.ds(at, step), :] - mean
        last = jnp.where(row + at == 0, 0.0, minus[pl.ds(at, step), :] - mean)
        even[pl.ds(at, step), :] = (first + last).astype(BF16)
        odd[pl.ds(at, step), :] = (first - last).astype(BF16)
        return carry

    lax.fori_loop(0, STEPS, two, 0, unroll=unroll)
    sign = (1 - 2 * (row % 2)).astype(F32)
    gain = math.sqrt(1.0 / half)

    def three(t, carry):
        at = pl.multiple_of(t * step, step)
        cosine = jnp.dot(cos_ref[pl.ds(at, step), :], even[...], preferred_element_type=F32)
        coeffs[pl.ds(at, step), :] = (gain * (cosine + sign * centre)).astype(BF16)
        sine = jnp.dot(sin_ref[pl.ds(at, step), :], odd[...], preferred_element_type=F32)
        coeffs[pl.ds(total + at, step), :] = (gain * sine).astype(BF16)
        return carry

    lax.fori_loop(0, STEPS, three, 0, unroll=unroll)
    for i, s in enumerate(order):
        at = pl.multiple_of((pos ^ s) * waves, 8)
        for r in range(2):
            for c in range(count):
                part = coeffs[pl.ds(r * total + at, waves), c * lanes : (c + 1) * lanes]
                outs[i][c, r] = part


def on_grid(pos, cosine, sine, middle, mix, coef, blocks, unroll):
    devices = len(blocks)
    pairs, _, waves, lanes = blocks[0].shape
    half, total = cosine.shape
    assert half == total == devices * waves
    count = 2 if pairs % 2 == 0 else 1
    width = count * lanes
    block = pl.BlockSpec((count, 2, waves, lanes), lambda q, s: (q, 0, 0, 0))
    whole = lambda q, s: (0, 0)
    return pl.pallas_call(
        functools.partial(grid_kernel, devices, waves, unroll),
        grid_spec=pltpu.PrefetchScalarGridSpec(
            num_scalar_prefetch=1,
            grid=(pairs // count,),
            in_specs=[
                pl.BlockSpec((half, total), whole),
                pl.BlockSpec((half, total), whole),
                pl.BlockSpec((8, total), whole),
                pl.BlockSpec((lanes, lanes), whole),
                pl.BlockSpec((2, lanes), whole),
            ]
            + [block] * devices,
            out_specs=[block] * devices + [pl.BlockSpec((1, 8, width), lambda q, s: (q, 0, 0))],
            scratch_shapes=[
                pltpu.VMEM((2 * total, width), BF16),
                pltpu.VMEM((half, width), F32),
                pltpu.VMEM((half, width), F32),
                pltpu.VMEM((half, width), BF16),
                pltpu.VMEM((half, width), BF16),
            ],
        ),
        out_shape=[jax.ShapeDtypeStruct(blocks[0].shape, BF16)] * devices
        + [jax.ShapeDtypeStruct((pairs // count, 8, width), F32)],
        compiler_params=params(),
        name="grid",
    )(pos, cosine, sine, middle, mix, coef, *blocks)


def inverse_kernel(
    devices, group, waves, unroll, pos_ref, sums_ref, spec_ref, basis_ref, trunc_ref, weight_ref, perm_ref,
    share_ref, *rest
):
    blocks = rest[:devices]
    out_ref, fold = rest[devices], rest[devices + 1 :]
    pos = pos_ref[0]
    levels = blocks[0].shape[3] // 4
    half_slots = spec_ref.shape[3]
    jj = perm_ref.shape[0] // 2
    pairs = jj // devices
    tiles = 4 * levels // LANES
    size = pairs * group
    for i, s in enumerate(exchange_order(devices)):
        at = pl.multiple_of((pos ^ s) * size, 8)
        for r in range(2):
            for t in range(tiles):
                block = blocks[i][:, r, :, t * LANES : (t + 1) * LANES].astype(F32)
                fold[r * tiles + t][pl.ds(at, size), :] = block.reshape(size, LANES)
    first = pos * waves + pl.program_id(0) * group
    slot = 2 * lax.broadcasted_iota(jnp.int32, (1, half_slots), 1)
    trunc = trunc_ref[...]
    weight = weight_ref[...]

    def one(m, carry):
        wave = first + m
        turned = []
        for r in range(2):
            at = pl.ds(m, jj, stride=group)
            total = sums_ref[r * waves + pl.program_id(0) * group + m]
            columns = []
            for t in range(tiles):
                share = total * share_ref[:, t * LANES : (t + 1) * LANES]
                columns.append((fold[r * tiles + t][at, :] + share).T)
            turned.append(jnp.concatenate(columns, axis=0))
        rows = []
        for hemi in range(2):
            for r in range(2):
                pieces = []
                for half in range(2):
                    at = (2 * half + hemi) * levels
                    pieces.append(turned[r][at : at + levels])
                rows.append(jnp.concatenate(pieces, axis=1))
        both = jnp.concatenate(rows, axis=0).astype(BF16)
        both = jnp.dot(both, perm_ref[...], preferred_element_type=F32)
        both = jnp.where(trunc > wave, both, 0.0)
        channels = 2 * levels
        north, south = both[:channels], both[channels:]
        for p in range(2):
            folded = (weight * (north + south if p == 0 else north - south)).astype(BF16)
            direct = lax.dot_general(
                folded, basis_ref[m, p], (((1,), (1,)), ((), ())), preferred_element_type=F32
            )
            value = spec_ref[m, p].astype(F32) + direct
            out_ref[m, p] = jnp.where(slot + (wave + p) < 2 * half_slots, value, 0.0).astype(BF16)
        return carry

    lax.fori_loop(0, group, one, 0, unroll=min(group, unroll))


def inverse(pos, sums, spec, basis, trunc, weight, perm, share, blocks, unroll):
    devices = len(blocks)
    waves, _, channels, half_slots = spec.shape
    half_lats = basis.shape[3]
    group = min(8, waves)
    pairs = half_lats // (2 * devices)
    lanes = 2 * channels
    return pl.pallas_call(
        functools.partial(inverse_kernel, devices, group, waves, unroll),
        grid_spec=pltpu.PrefetchScalarGridSpec(
            num_scalar_prefetch=1,
            grid=(waves // group,),
            in_specs=[
                pl.BlockSpec(memory_space=pltpu.SMEM),
                pl.BlockSpec((group, 2, channels, half_slots), lambda i, s: (i, 0, 0, 0)),
                pl.BlockSpec((group, 2, half_slots, half_lats), lambda i, s: (i, 0, 0, 0)),
                pl.BlockSpec((1, half_lats), lambda i, s: (0, 0)),
                pl.BlockSpec((1, half_lats), lambda i, s: (0, 0)),
                pl.BlockSpec((half_lats, half_lats), lambda i, s: (0, 0)),
                pl.BlockSpec((half_lats // 2, lanes), lambda i, s: (0, 0)),
            ]
            + [pl.BlockSpec((pairs, 2, group, lanes), lambda i, s: (0, 0, i, 0))] * devices,
            out_specs=pl.BlockSpec((group, 2, channels, half_slots), lambda i, s: (i, 0, 0, 0)),
            scratch_shapes=[pltpu.VMEM((half_lats // 2 * group, LANES), F32)] * (2 * lanes // LANES),
        ),
        out_shape=jax.ShapeDtypeStruct(spec.shape, BF16),
        compiler_params=params(),
        name="inverse",
    )(pos, sums, spec, basis, trunc, weight, perm, share, *blocks)


def cos_sin(rows, columns):
    phases = rows[:, None] * columns[None, :] % NLON
    angles = phases.astype(F32) * (2.0 * math.pi / NLON)
    return jnp.cos(angles), jnp.sin(angles)


def fourier_tables(size):
    low = 32
    col = jnp.arange(size, dtype=jnp.int32)
    c0, s0, c1, s1 = lax.optimization_barrier(
        cos_sin(jnp.arange(low, dtype=jnp.int32), col)
        + cos_sin(low * jnp.arange(size // low, dtype=jnp.int32), col)
    )
    cos = c1[:, None] * c0[None] - s1[:, None] * s0[None]
    sin = s1[:, None] * c0[None] + c1[:, None] * s0[None]
    return cos.reshape(size, size).astype(BF16), (-sin).reshape(size, size).astype(BF16)


def exchange(arrays, devices, needed, relay=False):
    quarter = devices // 4
    hop = quarter // 2
    far = 3 * quarter + hop
    handed = [d for d in range(devices) if relay and hop and not d & hop and needed(d, d ^ far)]
    order = exchange_order(devices)
    if handed:
        moved = lax.ppermute(arrays[order.index(far)], "wave", [(d, d ^ hop) for d in handed])
        moved = lax.ppermute(moved, "wave", [(d ^ hop, d ^ far) for d in handed])
    got = [arrays[0]]
    for array, s in list(zip(arrays, order))[1:]:
        skip = handed if s == far else []
        pairs = [(i, i ^ s) for i in range(devices) if needed(i, i ^ s) and i not in skip]
        array = lax.ppermute(array, "wave", pairs)
        got.append(array + moved if skip else array)
    return got


def per_device(spectral, basis, quad_weights, column, square_coef, cube_coef, trunc):
    devices = lax.axis_size("wave")
    position = lax.axis_index("wave").astype(jnp.int32)
    waves, _, _, channels = spectral.shape
    half_lats = basis.shape[3]
    levels = channels // 2
    rows = half_lats // devices
    pairs = rows // 2
    pos = position.reshape(1)
    spec = jnp.swapaxes(spectral, 2, 3)
    order = latitude_order(half_lats, devices)
    lats = jnp.arange(half_lats, dtype=jnp.int32)
    perm = (lats[:, None] == order[None, :]).astype(BF16)
    back = (order[:, None] == lats[None, :]).astype(BF16)
    trunc_row = trunc.reshape(1, half_lats)
    weight_row = quad_weights.reshape(1, half_lats)
    blocks = forward(pos, spec, basis, trunc_row, perm, devices)

    groups = owned_groups(devices)
    reach = [min(devices, g + 1 + max(1, devices // 16)) for g in range(devices)]
    fits = jnp.all(trunc <= jnp.array(np.repeat(waves * np.array(reach, np.int32), rows)))

    def finish(sparse, blocks):
        def there(source, owner):
            return not sparse or source < reach[groups[owner]]

        def home(owner, source):
            return there(source, owner)

        total = devices * waves
        cosine, sine = fourier_tables(total)
        sign = 1 - 2 * (jnp.arange(total, dtype=jnp.int32) % 2)
        middle = jnp.broadcast_to(sign.astype(BF16), (8, total))
        mix = jnp.kron(jnp.eye(4, dtype=F32), column.T).astype(BF16)
        coef = jnp.stack([jnp.tile(square_coef, 4), jnp.tile(cube_coef, 4)])
        sums = 2.0 * jnp.sum(cosine.astype(F32), axis=1) - cosine[:, 0].astype(F32)
        sums = jnp.stack([sums + sign.astype(F32), jnp.zeros((total,), F32)])
        kept = lax.dynamic_slice(sums, (0, position * waves), (2, waves)).reshape(-1)
        held = quad_weights.reshape(devices, 2, pairs)
        held = jnp.swapaxes(jnp.stack([held[g] for g in groups]), 1, 2)
        held = held.reshape(devices * pairs, 2, 1, 1) / (2.0 * jnp.sum(quad_weights))

        got = exchange(blocks, devices, there, relay=sparse)
        *parts, means = on_grid(
            pos, cosine, sine, middle, mix, coef, got, STEPS if sparse else 1
        )
        parts = exchange(parts, devices, home)

        sent = means[:, 0].reshape(1, -1, LANES)
        sent = jnp.broadcast_to(sent, (devices,) + sent.shape[1:])
        every = lax.all_to_all(sent, "wave", split_axis=0, concat_axis=0, tiled=True)
        every = every.reshape(devices * pairs, 4 * levels)
        level_mean = jnp.sum(held * every.reshape(-1, 2, 2, levels), axis=(0, 1, 2))
        share = math.sqrt(2.0 / NLON) * (every - jnp.tile(level_mean, 4))
        return inverse(
            pos, kept, spec, basis, trunc_row, weight_row, back, share, parts,
            8 if sparse else 1,
        )

    def sparse(blocks):
        return finish(True, blocks)

    def dense(blocks):
        return finish(False, blocks)

    out = lax.cond(fits, sparse, dense, blocks)
    return jnp.swapaxes(out, 2, 3)


def solution(mesh):
    return jax.shard_map(
        per_device,
        mesh=mesh,
        in_specs=(
            P(("member", "wave"), None, None, None),
            P("wave", None, None, None),
            P(),
            P(),
            P(),
            P(),
            P(),
        ),
        out_specs=P(("member", "wave"), None, None, None),
        check_vma=False,
    )
```

```python
import functools
import math

import jax
import jax.numpy as jnp
import numpy as np
from jax import lax
from jax.experimental import pallas as pl
from jax.experimental.pallas import tpu as pltpu
from jax.sharding import PartitionSpec as P


NLON = 1024
LANES = 128
F32 = jnp.float32
BF16 = jnp.bfloat16
STEPS = 2
VMEM_LIMIT = 56 * 1024 * 1024


def params():
    return pltpu.CompilerParams(
        dimension_semantics=("arbitrary",), vmem_limit_bytes=VMEM_LIMIT
    )


def owned_groups(devices):
    turn = (0, 3, 1, 2) if devices % 4 == 0 else tuple(range(devices))
    size = len(turn)
    return [devices - 1 - (e // size * size + turn[e % size]) for e in range(devices)]


def latitude_order(half_lats, devices):
    rows = half_lats // devices
    pairs = rows // 2
    lane = np.arange(half_lats)
    half = lane // (half_lats // 2)
    owner = lane % (half_lats // 2) // pairs
    group = np.array(owned_groups(devices))[owner]
    return (group * rows + half * pairs + lane % pairs).astype(np.int32)


def exchange_order(devices):
    quarter = max(1, devices // 4)
    order = [0]
    for t in range(quarter):
        order += [2 * quarter + t, quarter + t, 3 * quarter + t]
        order += [quarter - 1 - t] if t < quarter - 1 else []
    return order


def forward_kernel(devices, group, waves, pos_ref, spec_ref, basis_ref, trunc_ref, perm_ref, *rest):
    outs, fold = rest[:devices], rest[devices:]
    pos = pos_ref[0]
    levels = outs[0].shape[3] // 4
    half_slots = spec_ref.shape[3]
    tiles = 4 * levels // LANES
    jj = perm_ref.shape[1] // 2
    pairs = jj // devices
    first = pos * waves + pl.program_id(0) * group
    slot = 2 * lax.broadcasted_iota(jnp.int32, (1, half_slots), 1)
    trunc = trunc_ref[...]

    def one(m, carry):
        wave = first + m
        parity = []
        for p in range(2):
            spec = spec_ref[m, p]
            spec = jnp.where(slot + (wave + p) < 2 * half_slots, spec, jnp.zeros_like(spec))
            parity.append(jnp.dot(spec, basis_ref[m, p], preferred_element_type=F32))
        both = jnp.concatenate([parity[0] + parity[1], parity[0] - parity[1]], axis=0)
        both = jnp.where(trunc > wave, both, 0.0).astype(BF16)
        both = jnp.dot(both, perm_ref[...], preferred_element_type=F32)
        for r in range(2):
            rows = []
            for half in range(2):
                for hemi in range(2):
                    at = (2 * hemi + r) * levels
                    rows.append(both[at : at + levels, half * jj : (half + 1) * jj])
            turned = jnp.concatenate(rows, axis=0).T
            for t in range(tiles):
                at = pl.ds(m, jj, stride=group)
                fold[r * tiles + t][at, :] = turned[:, t * LANES : (t + 1) * LANES]
        return carry

    lax.fori_loop(0, group, one, 0, unroll=group)
    size = pairs * group
    for i, s in enumerate(exchange_order(devices)):
        at = pl.multiple_of((pos ^ s) * size, 8)
        for r in range(2):
            for t in range(tiles):
                block = fold[r * tiles + t][pl.ds(at, size), :].reshape(pairs, group, LANES)
                outs[i][:, r, :, t * LANES : (t + 1) * LANES] = block.astype(BF16)


def forward(pos, spec, basis, trunc, perm, devices):
    waves, _, channels, half_slots = spec.shape
    half_lats = basis.shape[3]
    group = min(8, waves)
    pairs = half_lats // (2 * devices)
    lanes = 2 * channels
    return pl.pallas_call(
        functools.partial(forward_kernel, devices, group, waves),
        grid_spec=pltpu.PrefetchScalarGridSpec(
            num_scalar_prefetch=1,
            grid=(waves // group,),
            in_specs=[
                pl.BlockSpec((group, 2, channels, half_slots), lambda i, s: (i, 0, 0, 0)),
                pl.BlockSpec((group, 2, half_slots, half_lats), lambda i, s: (i, 0, 0, 0)),
                pl.BlockSpec((1, half_lats), lambda i, s: (0, 0)),
                pl.BlockSpec((half_lats, half_lats), lambda i, s: (0, 0)),
            ],
            out_specs=[pl.BlockSpec((pairs, 2, group, lanes), lambda i, s: (0, 0, i, 0))] * devices,
            scratch_shapes=[pltpu.VMEM((half_lats // 2 * group, LANES), F32)] * (2 * lanes // LANES),
        ),
        out_shape=[jax.ShapeDtypeStruct((pairs, 2, waves, lanes), BF16)] * devices,
        compiler_params=params(),
        name="forward",
    )(pos, spec, basis, trunc, perm)


def grid_kernel(devices, waves, unroll, pos_ref, cos_ref, sin_ref, mid_ref, mix_ref, coef_ref, *rest):
    blocks, outs = rest[:devices], rest[devices : 2 * devices]
    mean_ref, coeffs, plus, minus, even, odd = rest[2 * devices :]
    pos = pos_ref[0]
    total = devices * waves
    count, lanes = blocks[0].shape[0], blocks[0].shape[3]
    width = count * lanes
    order = exchange_order(devices)
    for i, s in enumerate(order):
        at = pl.multiple_of((pos ^ s) * waves, 8)
        for r in range(2):
            for c in range(count):
                part = blocks[i][c, r]
                coeffs[pl.ds(r * total + at, waves), c * lanes : (c + 1) * lanes] = part
    half = cos_ref.shape[0]
    step = half // STEPS
    scale = 1.0 / math.sqrt(total)
    middle = jnp.dot(mid_ref[...], coeffs[:total, :], preferred_element_type=F32)[0:1]
    row = lax.broadcasted_iota(jnp.int32, (step, 1), 0)

    def tendency(temp):
        values = []
        for c in range(count):
            mine = temp[:, c * lanes : (c + 1) * lanes]
            mixed = jnp.dot(mine.astype(BF16), mix_ref[...], preferred_element_type=F32)
            values.append(mixed + mine * mine * (coef_ref[0:1, :] - coef_ref[1:2, :] * mine))
        return jnp.concatenate(values, axis=1)

    def one(t, total_sum):
        at = pl.multiple_of(t * step, step)
        cosine = jnp.dot(
            cos_ref[pl.ds(at, step), :], coeffs[:total, :], preferred_element_type=F32
        )
        sine = jnp.dot(
            sin_ref[pl.ds(at, step), :], coeffs[total:, :], preferred_element_type=F32
        )
        first = tendency(scale * (cosine + sine))
        last = tendency(scale * jnp.where(row + at == 0, middle, cosine - sine))
        plus[pl.ds(at, step), :] = first
        minus[pl.ds(at, step), :] = last
        return total_sum + jnp.sum(first + last, axis=0, keepdims=True)

    mean = lax.fori_loop(0, STEPS, one, jnp.zeros((1, width), F32), unroll=unroll)
    mean = mean * (0.5 / half)
    mean_ref[0] = jnp.broadcast_to(mean, mean_ref.shape[1:])
    centre = minus[0:1, :] - mean

    def two(t, carry):
        at = pl.multiple_of(t * step, step)
        first = plus[pl.ds(at, step), :] - mean
        last = jnp.where(row + at == 0, 0.0, minus[pl.ds(at, step), :] - mean)
        even[pl.ds(at, step), :] = (first + last).astype(BF16)
        odd[pl.ds(at, step), :] = (first - last).astype(BF16)
        return carry

    lax.fori_loop(0, STEPS, two, 0, unroll=unroll)
    sign = (1 - 2 * (row % 2)).astype(F32)
    gain = math.sqrt(1.0 / half)

    def three(t, carry):
        at = pl.multiple_of(t * step, step)
        cosine = jnp.dot(cos_ref[pl.ds(at, step), :], even[...], preferred_element_type=F32)
        coeffs[pl.ds(at, step), :] = (gain * (cosine + sign * centre)).astype(BF16)
        sine = jnp.dot(sin_ref[pl.ds(at, step), :], odd[...], preferred_element_type=F32)
        coeffs[pl.ds(total + at, step), :] = (gain * sine).astype(BF16)
        return carry

    lax.fori_loop(0, STEPS, three, 0, unroll=unroll)
    for i, s in enumerate(order):
        at = pl.multiple_of((pos ^ s) * waves, 8)
        for r in range(2):
            for c in range(count):
                part = coeffs[pl.ds(r * total + at, waves), c * lanes : (c + 1) * lanes]
                outs[i][c, r] = part


def on_grid(pos, cosine, sine, middle, mix, coef, blocks, unroll):
    devices = len(blocks)
    pairs, _, waves, lanes = blocks[0].shape
    half, total = cosine.shape
    assert half == total == devices * waves
    count = 2 if pairs % 2 == 0 else 1
    width = count * lanes
    block = pl.BlockSpec((count, 2, waves, lanes), lambda q, s: (q, 0, 0, 0))
    whole = lambda q, s: (0, 0)
    return pl.pallas_call(
        functools.partial(grid_kernel, devices, waves, unroll),
        grid_spec=pltpu.PrefetchScalarGridSpec(
            num_scalar_prefetch=1,
            grid=(pairs // count,),
            in_specs=[
                pl.BlockSpec((half, total), whole),
                pl.BlockSpec((half, total), whole),
                pl.BlockSpec((8, total), whole),
                pl.BlockSpec((lanes, lanes), whole),
                pl.BlockSpec((2, lanes), whole),
            ]
            + [block] * devices,
            out_specs=[block] * devices + [pl.BlockSpec((1, 8, width), lambda q, s: (q, 0, 0))],
            scratch_shapes=[
                pltpu.VMEM((2 * total, width), BF16),
                pltpu.VMEM((half, width), F32),
                pltpu.VMEM((half, width), F32),
                pltpu.VMEM((half, width), BF16),
                pltpu.VMEM((half, width), BF16),
            ],
        ),
        out_shape=[jax.ShapeDtypeStruct(blocks[0].shape, BF16)] * devices
        + [jax.ShapeDtypeStruct((pairs // count, 8, width), F32)],
        compiler_params=params(),
        name="grid",
    )(pos, cosine, sine, middle, mix, coef, *blocks)


def inverse_kernel(
    devices, group, waves, unroll, pos_ref, sums_ref, spec_ref, basis_ref, trunc_ref, weight_ref, perm_ref,
    share_ref, *rest
):
    blocks = rest[:devices]
    out_ref, fold = rest[devices], rest[devices + 1 :]
    pos = pos_ref[0]
    levels = blocks[0].shape[3] // 4
    half_slots = spec_ref.shape[3]
    jj = perm_ref.shape[0] // 2
    pairs = jj // devices
    tiles = 4 * levels // LANES
    size = pairs * group
    for i, s in enumerate(exchange_order(devices)):
        at = pl.multiple_of((pos ^ s) * size, 8)
        for r in range(2):
            for t in range(tiles):
                block = blocks[i][:, r, :, t * LANES : (t + 1) * LANES].astype(F32)
                fold[r * tiles + t][pl.ds(at, size), :] = block.reshape(size, LANES)
    first = pos * waves + pl.program_id(0) * group
    slot = 2 * lax.broadcasted_iota(jnp.int32, (1, half_slots), 1)
    trunc = trunc_ref[...]
    weight = weight_ref[...]

    def one(m, carry):
        wave = first + m
        turned = []
        for r in range(2):
            at = pl.ds(m, jj, stride=group)
            total = sums_ref[r * waves + pl.program_id(0) * group + m]
            columns = []
            for t in range(tiles):
                share = total * share_ref[:, t * LANES : (t + 1) * LANES]
                columns.append((fold[r * tiles + t][at, :] + share).T)
            turned.append(jnp.concatenate(columns, axis=0))
        rows = []
        for hemi in range(2):
            for r in range(2):
                pieces = []
                for half in range(2):
                    at = (2 * half + hemi) * levels
                    pieces.append(turned[r][at : at + levels])
                rows.append(jnp.concatenate(pieces, axis=1))
        both = jnp.concatenate(rows, axis=0).astype(BF16)
        both = jnp.dot(both, perm_ref[...], preferred_element_type=F32)
        both = jnp.where(trunc > wave, both, 0.0)
        channels = 2 * levels
        north, south = both[:channels], both[channels:]
        for p in range(2):
            folded = (weight * (north + south if p == 0 else north - south)).astype(BF16)
            direct = lax.dot_general(
                folded, basis_ref[m, p], (((1,), (1,)), ((), ())), preferred_element_type=F32
            )
            value = spec_ref[m, p].astype(F32) + direct
            out_ref[m, p] = jnp.where(slot + (wave + p) < 2 * half_slots, value, 0.0).astype(BF16)
        return carry

    lax.fori_loop(0, group, one, 0, unroll=min(group, unroll))


def inverse(pos, sums, spec, basis, trunc, weight, perm, share, blocks, unroll):
    devices = len(blocks)
    waves, _, channels, half_slots = spec.shape
    half_lats = basis.shape[3]
    group = min(8, waves)
    pairs = half_lats // (2 * devices)
    lanes = 2 * channels
    return pl.pallas_call(
        functools.partial(inverse_kernel, devices, group, waves, unroll),
        grid_spec=pltpu.PrefetchScalarGridSpec(
            num_scalar_prefetch=1,
            grid=(waves // group,),
            in_specs=[
                pl.BlockSpec(memory_space=pltpu.SMEM),
                pl.BlockSpec((group, 2, channels, half_slots), lambda i, s: (i, 0, 0, 0)),
                pl.BlockSpec((group, 2, half_slots, half_lats), lambda i, s: (i, 0, 0, 0)),
                pl.BlockSpec((1, half_lats), lambda i, s: (0, 0)),
                pl.BlockSpec((1, half_lats), lambda i, s: (0, 0)),
                pl.BlockSpec((half_lats, half_lats), lambda i, s: (0, 0)),
                pl.BlockSpec((half_lats // 2, lanes), lambda i, s: (0, 0)),
            ]
            + [pl.BlockSpec((pairs, 2, group, lanes), lambda i, s: (0, 0, i, 0))] * devices,
            out_specs=pl.BlockSpec((group, 2, channels, half_slots), lambda i, s: (i, 0, 0, 0)),
            scratch_shapes=[pltpu.VMEM((half_lats // 2 * group, LANES), F32)] * (2 * lanes // LANES),
        ),
        out_shape=jax.ShapeDtypeStruct(spec.shape, BF16),
        compiler_params=params(),
        name="inverse",
    )(pos, sums, spec, basis, trunc, weight, perm, share, *blocks)


def cos_sin(rows, columns):
    phases = rows[:, None] * columns[None, :] % NLON
    angles = phases.astype(F32) * (2.0 * math.pi / NLON)
    return jnp.cos(angles), jnp.sin(angles)


def fourier_tables(size):
    low = 32
    col = jnp.arange(size, dtype=jnp.int32)
    c0, s0, c1, s1 = lax.optimization_barrier(
        cos_sin(jnp.arange(low, dtype=jnp.int32), col)
        + cos_sin(low * jnp.arange(size // low, dtype=jnp.int32), col)
    )
    cos = c1[:, None] * c0[None] - s1[:, None] * s0[None]
    sin = s1[:, None] * c0[None] + c1[:, None] * s0[None]
    return cos.reshape(size, size).astype(BF16), (-sin).reshape(size, size).astype(BF16)


def relay_shifts(devices):
    hop = devices // 8
    return hop, devices // 4 * 3 + hop


def exchange(arrays, devices, needed, relay=False):
    hop, far = relay_shifts(devices)
    handed = [d for d in range(devices) if relay and hop and not d & hop and needed(d, d ^ far)]
    order = exchange_order(devices)
    if handed:
        moved = lax.ppermute(arrays[order.index(far)], "wave", [(d, d ^ hop) for d in handed])
        moved = lax.ppermute(moved, "wave", [(d ^ hop, d ^ far) for d in handed])
    got = [arrays[0]]
    for array, s in list(zip(arrays, order))[1:]:
        skip = handed if s == far else []
        pairs = [(i, i ^ s) for i in range(devices) if needed(i, i ^ s) and i not in skip]
        array = lax.ppermute(array, "wave", pairs)
        got.append(array + moved if skip else array)
    return got


def per_device(spectral, basis, quad_weights, column, square_coef, cube_coef, trunc):
    devices = lax.axis_size("wave")
    position = lax.axis_index("wave").astype(jnp.int32)
    waves, _, _, channels = spectral.shape
    half_lats = basis.shape[3]
    levels = channels // 2
    rows = half_lats // devices
    pairs = rows // 2
    pos = position.reshape(1)
    spec = jnp.swapaxes(spectral, 2, 3)
    order = latitude_order(half_lats, devices)
    perm = np.eye(half_lats, dtype=BF16)[:, order]
    perm, back = jnp.array(perm), jnp.array(np.ascontiguousarray(perm.T))
    trunc_row = trunc.reshape(1, half_lats)
    weight_row = quad_weights.reshape(1, half_lats)
    blocks = forward(pos, spec, basis, trunc_row, perm, devices)

    groups = owned_groups(devices)
    reach = [min(devices, g + 1 + max(1, devices // 16)) for g in range(devices)]
    fits = jnp.all(trunc <= jnp.array(np.repeat(waves * np.array(reach, np.int32), rows)))

    def finish(sparse, blocks):
        def there(source, owner):
            return not sparse or source < reach[groups[owner]]

        def home(owner, source):
            return there(source, owner)

        total = devices * waves
        cosine, sine = fourier_tables(total)
        sign = 1 - 2 * (jnp.arange(total, dtype=jnp.int32) % 2)
        middle = jnp.array(np.tile(1 - 2 * (np.arange(total) % 2), (8, 1)).astype(BF16))
        mix = jnp.kron(jnp.eye(4, dtype=F32), column.T).astype(BF16)
        coef = jnp.stack([jnp.tile(square_coef, 4), jnp.tile(cube_coef, 4)])
        sums = 2.0 * jnp.sum(cosine.astype(F32), axis=1) - cosine[:, 0].astype(F32)
        sums = jnp.stack([sums + sign.astype(F32), jnp.zeros((total,), F32)])
        kept = lax.dynamic_slice(sums, (0, position * waves), (2, waves)).reshape(-1)
        held = quad_weights.reshape(devices, 2, pairs)
        held = jnp.swapaxes(jnp.stack([held[g] for g in groups]), 1, 2)
        held = held.reshape(devices * pairs, 2, 1, 1) / (2.0 * jnp.sum(quad_weights))

        got = exchange(blocks, devices, there, relay=sparse)
        *parts, means = on_grid(
            pos, cosine, sine, middle, mix, coef, got, STEPS if sparse else 1
        )
        parts = exchange(parts, devices, home)

        sent = means[:, 0].reshape(1, -1, LANES)
        sent = jnp.broadcast_to(sent, (devices,) + sent.shape[1:])
        every = lax.all_to_all(sent, "wave", split_axis=0, concat_axis=0, tiled=True)
        every = every.reshape(devices * pairs, 4 * levels)
        level_mean = jnp.sum(held * every.reshape(-1, 2, 2, levels), axis=(0, 1, 2))
        share = math.sqrt(2.0 / NLON) * (every - jnp.tile(level_mean, 4))
        return inverse(
            pos, kept, spec, basis, trunc_row, weight_row, back, share, parts,
            8 if sparse else 1,
        )

    def sparse(blocks):
        return finish(True, blocks)

    def dense(blocks):
        return finish(False, blocks)

    out = lax.cond(fits, sparse, dense, blocks)
    return jnp.swapaxes(out, 2, 3)


def solution(mesh):
    return jax.shard_map(
        per_device,
        mesh=mesh,
        in_specs=(
            P(("member", "wave"), None, None, None),
            P("wave", None, None, None),
            P(),
            P(),
            P(),
            P(),
            P(),
        ),
        out_specs=P(("member", "wave"), None, None, None),
        check_vma=False,
    )
```

```python
import functools
import math

import jax
import jax.numpy as jnp
import numpy as np
from jax import lax
from jax.experimental import pallas as pl
from jax.experimental.pallas import tpu as pltpu
from jax.sharding import PartitionSpec as P


NLON = 1024
LANES = 128
F32 = jnp.float32
BF16 = jnp.bfloat16
STEPS = 2
VMEM_LIMIT = 56 * 1024 * 1024


def params():
    return pltpu.CompilerParams(
        dimension_semantics=("arbitrary",), vmem_limit_bytes=VMEM_LIMIT
    )


def owned_groups(devices):
    turn = (0, 3, 1, 2) if devices % 4 == 0 else tuple(range(devices))
    size = len(turn)
    return [devices - 1 - (e // size * size + turn[e % size]) for e in range(devices)]


def latitude_order(half_lats, devices):
    rows = half_lats // devices
    pairs = rows // 2
    lane = np.arange(half_lats)
    half = lane // (half_lats // 2)
    owner = lane % (half_lats // 2) // pairs
    group = np.array(owned_groups(devices))[owner]
    return (group * rows + half * pairs + lane % pairs).astype(np.int32)


def exchange_order(devices):
    quarter = max(1, devices // 4)
    order = [0]
    for t in range(quarter):
        order += [2 * quarter + t, quarter + t, 3 * quarter + t]
        order += [quarter - 1 - t] if t < quarter - 1 else []
    return order


def forward_kernel(devices, group, waves, pos_ref, spec_ref, basis_ref, trunc_ref, perm_ref, *rest):
    outs, fold = rest[:devices], rest[devices:]
    pos = pos_ref[0]
    levels = outs[0].shape[3] // 4
    half_slots = spec_ref.shape[3]
    tiles = 4 * levels // LANES
    jj = perm_ref.shape[1] // 2
    pairs = jj // devices
    first = pos * waves + pl.program_id(0) * group
    slot = 2 * lax.broadcasted_iota(jnp.int32, (1, half_slots), 1)
    trunc = trunc_ref[...]

    def one(m, carry):
        wave = first + m
        parity = []
        for p in range(2):
            spec = spec_ref[m, p]
            spec = jnp.where(slot + (wave + p) < 2 * half_slots, spec, jnp.zeros_like(spec))
            parity.append(jnp.dot(spec, basis_ref[m, p], preferred_element_type=F32))
        both = jnp.concatenate([parity[0] + parity[1], parity[0] - parity[1]], axis=0)
        both = jnp.where(trunc > wave, both, 0.0).astype(BF16)
        both = jnp.dot(both, perm_ref[...], preferred_element_type=F32)
        for r in range(2):
            rows = []
            for half in range(2):
                for hemi in range(2):
                    at = (2 * hemi + r) * levels
                    rows.append(both[at : at + levels, half * jj : (half + 1) * jj])
            turned = jnp.concatenate(rows, axis=0).T
            for t in range(tiles):
                at = pl.ds(m, jj, stride=group)
                fold[r * tiles + t][at, :] = turned[:, t * LANES : (t + 1) * LANES]
        return carry

    lax.fori_loop(0, group, one, 0, unroll=group)
    size = pairs * group
    for i, s in enumerate(exchange_order(devices)):
        at = pl.multiple_of((pos ^ s) * size, 8)
        for r in range(2):
            for t in range(tiles):
                block = fold[r * tiles + t][pl.ds(at, size), :].reshape(pairs, group, LANES)
                outs[i][:, r, :, t * LANES : (t + 1) * LANES] = block.astype(BF16)


def forward(pos, spec, basis, trunc, perm, devices):
    waves, _, channels, half_slots = spec.shape
    half_lats = basis.shape[3]
    group = min(8, waves)
    pairs = half_lats // (2 * devices)
    lanes = 2 * channels
    return pl.pallas_call(
        functools.partial(forward_kernel, devices, group, waves),
        grid_spec=pltpu.PrefetchScalarGridSpec(
            num_scalar_prefetch=1,
            grid=(waves // group,),
            in_specs=[
                pl.BlockSpec((group, 2, channels, half_slots), lambda i, s: (i, 0, 0, 0)),
                pl.BlockSpec((group, 2, half_slots, half_lats), lambda i, s: (i, 0, 0, 0)),
                pl.BlockSpec((1, half_lats), lambda i, s: (0, 0)),
                pl.BlockSpec((half_lats, half_lats), lambda i, s: (0, 0)),
            ],
            out_specs=[pl.BlockSpec((pairs, 2, group, lanes), lambda i, s: (0, 0, i, 0))] * devices,
            scratch_shapes=[pltpu.VMEM((half_lats // 2 * group, LANES), F32)] * (2 * lanes // LANES),
        ),
        out_shape=[jax.ShapeDtypeStruct((pairs, 2, waves, lanes), BF16)] * devices,
        compiler_params=params(),
        name="forward",
    )(pos, spec, basis, trunc, perm)


def grid_kernel(devices, waves, unroll, pos_ref, cos_ref, sin_ref, mid_ref, mix_ref, coef_ref, *rest):
    blocks, outs = rest[:devices], rest[devices : 2 * devices]
    mean_ref, coeffs, plus, minus, even, odd = rest[2 * devices :]
    pos = pos_ref[0]
    total = devices * waves
    count, lanes = blocks[0].shape[0], blocks[0].shape[3]
    width = count * lanes
    order = exchange_order(devices)
    for i, s in enumerate(order):
        at = pl.multiple_of((pos ^ s) * waves, 8)
        for r in range(2):
            for c in range(count):
                part = blocks[i][c, r]
                coeffs[pl.ds(r * total + at, waves), c * lanes : (c + 1) * lanes] = part
    half = cos_ref.shape[0]
    step = half // STEPS
    scale = 1.0 / math.sqrt(total)
    middle = jnp.dot(mid_ref[...], coeffs[:total, :], preferred_element_type=F32)[0:1]
    row = lax.broadcasted_iota(jnp.int32, (step, 1), 0)

    def tendency(temp):
        values = []
        for c in range(count):
            mine = temp[:, c * lanes : (c + 1) * lanes]
            mixed = jnp.dot(mine.astype(BF16), mix_ref[...], preferred_element_type=F32)
            values.append(mixed + mine * mine * (coef_ref[0:1, :] - coef_ref[1:2, :] * mine))
        return jnp.concatenate(values, axis=1)

    def one(t, total_sum):
        at = pl.multiple_of(t * step, step)
        cosine = jnp.dot(
            cos_ref[pl.ds(at, step), :], coeffs[:total, :], preferred_element_type=F32
        )
        sine = jnp.dot(
            sin_ref[pl.ds(at, step), :], coeffs[total:, :], preferred_element_type=F32
        )
        first = tendency(scale * (cosine + sine))
        last = tendency(scale * jnp.where(row + at == 0, middle, cosine - sine))
        plus[pl.ds(at, step), :] = first
        minus[pl.ds(at, step), :] = last
        return total_sum + jnp.sum(first + last, axis=0, keepdims=True)

    mean = lax.fori_loop(0, STEPS, one, jnp.zeros((1, width), F32), unroll=unroll)
    mean = mean * (0.5 / half)
    mean_ref[0] = mean
    centre = minus[0:1, :] - mean

    def two(t, carry):
        at = pl.multiple_of(t * step, step)
        first = plus[pl.ds(at, step), :] - mean
        last = jnp.where(row + at == 0, 0.0, minus[pl.ds(at, step), :] - mean)
        even[pl.ds(at, step), :] = (first + last).astype(BF16)
        odd[pl.ds(at, step), :] = (first - last).astype(BF16)
        return carry

    lax.fori_loop(0, STEPS, two, 0, unroll=unroll)
    sign = (1 - 2 * (row % 2)).astype(F32)
    gain = math.sqrt(1.0 / half)

    def three(t, carry):
        at = pl.multiple_of(t * step, step)
        cosine = jnp.dot(cos_ref[pl.ds(at, step), :], even[...], preferred_element_type=F32)
        coeffs[pl.ds(at, step), :] = (gain * (cosine + sign * centre)).astype(BF16)
        sine = jnp.dot(sin_ref[pl.ds(at, step), :], odd[...], preferred_element_type=F32)
        coeffs[pl.ds(total + at, step), :] = (gain * sine).astype(BF16)
        return carry

    lax.fori_loop(0, STEPS, three, 0, unroll=unroll)
    for i, s in enumerate(order):
        at = pl.multiple_of((pos ^ s) * waves, 8)
        for r in range(2):
            for c in range(count):
                part = coeffs[pl.ds(r * total + at, waves), c * lanes : (c + 1) * lanes]
                outs[i][c, r] = part


def on_grid(pos, cosine, sine, middle, mix, coef, blocks, unroll):
    devices = len(blocks)
    pairs, _, waves, lanes = blocks[0].shape
    half, total = cosine.shape
    assert half == total == devices * waves
    count = 2 if pairs % 2 == 0 else 1
    width = count * lanes
    block = pl.BlockSpec((count, 2, waves, lanes), lambda q, s: (q, 0, 0, 0))
    whole = lambda q, s: (0, 0)
    return pl.pallas_call(
        functools.partial(grid_kernel, devices, waves, unroll),
        grid_spec=pltpu.PrefetchScalarGridSpec(
            num_scalar_prefetch=1,
            grid=(pairs // count,),
            in_specs=[
                pl.BlockSpec((half, total), whole),
                pl.BlockSpec((half, total), whole),
                pl.BlockSpec((8, total), whole),
                pl.BlockSpec((lanes, lanes), whole),
                pl.BlockSpec((2, lanes), whole),
            ]
            + [block] * devices,
            out_specs=[block] * devices + [pl.BlockSpec((1, 1, width), lambda q, s: (q, 0, 0))],
            scratch_shapes=[
                pltpu.VMEM((2 * total, width), BF16),
                pltpu.VMEM((half, width), F32),
                pltpu.VMEM((half, width), F32),
                pltpu.VMEM((half, width), BF16),
                pltpu.VMEM((half, width), BF16),
            ],
        ),
        out_shape=[jax.ShapeDtypeStruct(blocks[0].shape, BF16)] * devices
        + [jax.ShapeDtypeStruct((pairs // count, 1, width), F32)],
        compiler_params=params(),
        name="grid",
    )(pos, cosine, sine, middle, mix, coef, *blocks)


def inverse_kernel(
    devices, group, waves, unroll, pos_ref, sums_ref, spec_ref, basis_ref, trunc_ref, weight_ref, perm_ref,
    share_ref, *rest
):
    blocks = rest[:devices]
    out_ref, fold = rest[devices], rest[devices + 1 :]
    pos = pos_ref[0]
    levels = blocks[0].shape[3] // 4
    half_slots = spec_ref.shape[3]
    jj = perm_ref.shape[0] // 2
    pairs = jj // devices
    tiles = 4 * levels // LANES
    size = pairs * group
    for i, s in enumerate(exchange_order(devices)):
        at = pl.multiple_of((pos ^ s) * size, 8)
        for r in range(2):
            for t in range(tiles):
                block = blocks[i][:, r, :, t * LANES : (t + 1) * LANES].astype(F32)
                fold[r * tiles + t][pl.ds(at, size), :] = block.reshape(size, LANES)
    first = pos * waves + pl.program_id(0) * group
    slot = 2 * lax.broadcasted_iota(jnp.int32, (1, half_slots), 1)
    trunc = trunc_ref[...]
    weight = weight_ref[...]

    def one(m, carry):
        wave = first + m
        turned = []
        for r in range(2):
            at = pl.ds(m, jj, stride=group)
            total = sums_ref[r * waves + pl.program_id(0) * group + m]
            columns = []
            for t in range(tiles):
                share = total * share_ref[:, t * LANES : (t + 1) * LANES]
                columns.append((fold[r * tiles + t][at, :] + share).T)
            turned.append(jnp.concatenate(columns, axis=0))
        rows = []
        for hemi in range(2):
            for r in range(2):
                pieces = []
                for half in range(2):
                    at = (2 * half + hemi) * levels
                    pieces.append(turned[r][at : at + levels])
                rows.append(jnp.concatenate(pieces, axis=1))
        both = jnp.concatenate(rows, axis=0).astype(BF16)
        both = jnp.dot(both, perm_ref[...], preferred_element_type=F32)
        both = jnp.where(trunc > wave, both, 0.0)
        channels = 2 * levels
        north, south = both[:channels], both[channels:]
        for p in range(2):
            folded = (weight * (north + south if p == 0 else north - south)).astype(BF16)
            direct = lax.dot_general(
                folded, basis_ref[m, p], (((1,), (1,)), ((), ())), preferred_element_type=F32
            )
            value = spec_ref[m, p].astype(F32) + direct
            out_ref[m, p] = jnp.where(slot + (wave + p) < 2 * half_slots, value, 0.0).astype(BF16)
        return carry

    lax.fori_loop(0, group, one, 0, unroll=min(group, unroll))


def inverse(pos, sums, spec, basis, trunc, weight, perm, share, blocks, unroll):
    devices = len(blocks)
    waves, _, channels, half_slots = spec.shape
    half_lats = basis.shape[3]
    group = min(8, waves)
    pairs = half_lats // (2 * devices)
    lanes = 2 * channels
    return pl.pallas_call(
        functools.partial(inverse_kernel, devices, group, waves, unroll),
        grid_spec=pltpu.PrefetchScalarGridSpec(
            num_scalar_prefetch=1,
            grid=(waves // group,),
            in_specs=[
                pl.BlockSpec(memory_space=pltpu.SMEM),
                pl.BlockSpec((group, 2, channels, half_slots), lambda i, s: (i, 0, 0, 0)),
                pl.BlockSpec((group, 2, half_slots, half_lats), lambda i, s: (i, 0, 0, 0)),
                pl.BlockSpec((1, half_lats), lambda i, s: (0, 0)),
                pl.BlockSpec((1, half_lats), lambda i, s: (0, 0)),
                pl.BlockSpec((half_lats, half_lats), lambda i, s: (0, 0)),
                pl.BlockSpec((half_lats // 2, lanes), lambda i, s: (0, 0)),
            ]
            + [pl.BlockSpec((pairs, 2, group, lanes), lambda i, s: (0, 0, i, 0))] * devices,
            out_specs=pl.BlockSpec((group, 2, channels, half_slots), lambda i, s: (i, 0, 0, 0)),
            scratch_shapes=[pltpu.VMEM((half_lats // 2 * group, LANES), F32)] * (2 * lanes // LANES),
        ),
        out_shape=jax.ShapeDtypeStruct(spec.shape, BF16),
        compiler_params=params(),
        name="inverse",
    )(pos, sums, spec, basis, trunc, weight, perm, share, *blocks)


def cos_sin(rows, columns):
    phases = rows[:, None] * columns[None, :] % NLON
    angles = phases.astype(F32) * (2.0 * math.pi / NLON)
    return jnp.cos(angles), jnp.sin(angles)


def fourier_tables(size):
    low = 32
    col = jnp.arange(size, dtype=jnp.int32)
    c0, s0, c1, s1 = lax.optimization_barrier(
        cos_sin(jnp.arange(low, dtype=jnp.int32), col)
        + cos_sin(low * jnp.arange(size // low, dtype=jnp.int32), col)
    )
    cos = c1[:, None] * c0[None] - s1[:, None] * s0[None]
    sin = s1[:, None] * c0[None] + c1[:, None] * s0[None]
    return cos.reshape(size, size).astype(BF16), (-sin).reshape(size, size).astype(BF16)


def relay_shifts(devices):
    hop = devices // 8
    return hop, devices // 4 * 3 + hop


def exchange(arrays, devices, needed, relay=False):
    hop, far = relay_shifts(devices)
    handed = [d for d in range(devices) if relay and hop and not d & hop and needed(d, d ^ far)]
    order = exchange_order(devices)
    if handed:
        moved = lax.ppermute(arrays[order.index(far)], "wave", [(d, d ^ hop) for d in handed])
        moved = lax.ppermute(moved, "wave", [(d ^ hop, d ^ far) for d in handed])
    got = [arrays[0]]
    for array, s in list(zip(arrays, order))[1:]:
        skip = handed if s == far else []
        pairs = [(i, i ^ s) for i in range(devices) if needed(i, i ^ s) and i not in skip]
        array = lax.ppermute(array, "wave", pairs)
        got.append(array + moved if skip else array)
    return got


def per_device(spectral, basis, quad_weights, column, square_coef, cube_coef, trunc):
    devices = lax.axis_size("wave")
    position = lax.axis_index("wave").astype(jnp.int32)
    waves, _, _, channels = spectral.shape
    half_lats = basis.shape[3]
    levels = channels // 2
    rows = half_lats // devices
    pairs = rows // 2
    pos = position.reshape(1)
    spec = jnp.swapaxes(spectral, 2, 3)
    order = latitude_order(half_lats, devices)
    perm = np.eye(half_lats, dtype=BF16)[:, order]
    perm, back = jnp.array(perm), jnp.array(np.ascontiguousarray(perm.T))
    trunc_row = trunc.reshape(1, half_lats)
    weight_row = quad_weights.reshape(1, half_lats)
    blocks = forward(pos, spec, basis, trunc_row, perm, devices)

    groups = owned_groups(devices)
    reach = [min(devices, g + 1 + max(1, devices // 16)) for g in range(devices)]
    fits = jnp.all(trunc <= jnp.array(np.repeat(waves * np.array(reach, np.int32), rows)))

    def finish(sparse, blocks):
        def there(source, owner):
            return not sparse or source < reach[groups[owner]]

        def home(owner, source):
            return there(source, owner)

        total = devices * waves
        cosine, sine = fourier_tables(total)
        sign = 1 - 2 * (jnp.arange(total, dtype=jnp.int32) % 2)
        middle = jnp.array(np.tile(1 - 2 * (np.arange(total) % 2), (8, 1)).astype(BF16))
        mix = jnp.kron(jnp.eye(4, dtype=F32), column.T).astype(BF16)
        coef = jnp.stack([jnp.tile(square_coef, 4), jnp.tile(cube_coef, 4)])
        sums = 2.0 * jnp.sum(cosine.astype(F32), axis=1) - cosine[:, 0].astype(F32)
        sums = jnp.stack([sums + sign.astype(F32), jnp.zeros((total,), F32)])
        kept = lax.dynamic_slice(sums, (0, position * waves), (2, waves)).reshape(-1)
        held = quad_weights.reshape(devices, 2, pairs)
        held = jnp.swapaxes(jnp.stack([held[g] for g in groups]), 1, 2)
        held = held.reshape(devices * pairs, 2, 1, 1) / (2.0 * jnp.sum(quad_weights))

        got = exchange(blocks, devices, there, relay=sparse)
        *parts, means = on_grid(
            pos, cosine, sine, middle, mix, coef, got, STEPS if sparse else 1
        )
        parts = exchange(parts, devices, home)

        sent = means.reshape(1, -1, LANES)
        sent = jnp.broadcast_to(sent, (devices,) + sent.shape[1:])
        every = lax.all_to_all(sent, "wave", split_axis=0, concat_axis=0, tiled=True)
        every = every.reshape(devices * pairs, 4 * levels)
        level_mean = jnp.sum(held * every.reshape(-1, 2, 2, levels), axis=(0, 1, 2))
        share = math.sqrt(2.0 / NLON) * (every - jnp.tile(level_mean, 4))
        return inverse(
            pos, kept, spec, basis, trunc_row, weight_row, back, share, parts,
            8 if sparse else 1,
        )

    def sparse(blocks):
        return finish(True, blocks)

    def dense(blocks):
        return finish(False, blocks)

    out = lax.cond(fits, sparse, dense, blocks)
    return jnp.swapaxes(out, 2, 3)


def solution(mesh):
    return jax.shard_map(
        per_device,
        mesh=mesh,
        in_specs=(
            P(("member", "wave"), None, None, None),
            P("wave", None, None, None),
            P(),
            P(),
            P(),
            P(),
            P(),
        ),
        out_specs=P(("member", "wave"), None, None, None),
        check_vma=False,
    )
```
